32 devices in a mesh: fsdp: 8 (over z, x), ctx: 2 (over y), tp: 2 (over core).
Axes of the slice: x: 2, y: 2, z: 4, core: 2. Of those that a mesh axis runs over, the one named last changes fastest.
Arguments:
- tokens: bfloat16 [16, 1024, 1024], P('fsdp', 'ctx'), may hold values from -6 to 6
- out_grad: bfloat16 [16, 1024, 1024], P('fsdp', 'ctx'), may hold values from -6 to 6
- norm_gains: bfloat16 [2, 1024], P(None, ('fsdp', 'ctx')), may hold values from 0.5 to 1.5
- query_weight: bfloat16 [1024, 512], P(('fsdp', 'ctx'), 'tp'), may hold values from -0.25 to 0.25
- key_value_matrix: bfloat16 [1024, 2, 128], P(('fsdp', 'ctx'), 'tp'), may hold values from -0.1875 to 0.1875
- output_weight: bfloat16 [512, 1024], P('tp', ('fsdp', 'ctx')), may hold values from -0.75 to 0.75
- mixer_weight: bfloat16 [1024, 24, 128], P(('fsdp', 'ctx'), 'tp'), may hold values from -0.1875 to 0.1875
- state_weight: bfloat16 [1024, 256], P(('fsdp', 'ctx')), may hold values from -0.1875 to 0.1875
- step_weight: bfloat16 [1024, 24], P(('fsdp', 'ctx'), 'tp'), may hold values from -0.1875 to 0.1875
- conv_inner: bfloat16 [5, 1536], P(None, 'tp'), may hold values from -2.5 to 2.5
- conv_state: bfloat16 [5, 256], replicated, may hold values from -2.5 to 2.5
- step_bias: bfloat16 [24], P('tp'), may hold values from -4.5 to -3
- decay_log: bfloat16 [24], P('tp'), may hold values from -2.5 to 1
- skip_scale: bfloat16 [24], P('tp'), may hold values from 0.5 to 1.5
- gated_gain: bfloat16 [1536], P('tp'), may hold values from 0.5 to 1.5
- mamba_weight: bfloat16 [1536, 1024], P('tp', ('fsdp', 'ctx')), may hold values from -0.15625 to 0.15625
- gateup_weight: bfloat16 [1024, 2, 2048], P(('fsdp', 'ctx'), None, 'tp'), may hold values from -0.1875 to 0.1875
- down_weight: bfloat16 [2048, 1024], P('tp', ('fsdp', 'ctx')), may hold values from -0.125 to 0.125
Outputs:
- layer_out: bfloat16 [16, 1024, 1024], P('fsdp', 'ctx', 'tp')
- tokens_grad: float32 [16, 1024, 1024], P('fsdp', 'ctx')
- norm_gains_grad: float32 [2, 1024], P(None, ('fsdp', 'ctx'))
- query_weight_grad: float32 [1024, 512], P(('fsdp', 'ctx'), 'tp')
- keyvalue_weight_grad: float32 [1024, 2, 128], P(('fsdp', 'ctx'), 'tp')
- output_weight_grad: float32 [512, 1024], P('tp', ('fsdp', 'ctx'))
- mixer_weight_grad: float32 [1024, 24, 128], P(('fsdp', 'ctx'), 'tp')
- state_weight_grad: float32 [1024, 256], P(('fsdp', 'ctx'))
- step_weight_grad: float32 [1024, 24], P(('fsdp', 'ctx'), 'tp')
- conv_inner_grad: float32 [5, 1536], P(None, 'tp')
- conv_state_grad: float32 [5, 256], replicated
- step_bias_grad: float32 [24], P('tp')
- decay_log_grad: float32 [24], P('tp')
- skip_scale_grad: float32 [24], P('tp')
- gated_gain_grad: float32 [1536], P('tp')
- mamba_weight_grad: float32 [1536, 1024], P('tp', ('fsdp', 'ctx'))
- gateup_weight_grad: float32 [1024, 2, 2048], P(('fsdp', 'ctx'), None, 'tp')
- down_weight_grad: float32 [2048, 1024], P('tp', ('fsdp', 'ctx'))
The draws below stay inside these ranges and needn't reach their ends.
All inputs are finite; a program needn't handle non-finite values.
Results may differ from the reference program's by a relative error of at most 0.017.
Values may be sent and summed in bfloat16 or wider, within the bound.
No kernel may reach another device: no remote copies, remote signals or barrier semaphores. Data moves between devices by JAX's collectives and lax.ppermute only.
A program may use at most 320 MiB of HBM per device.

```python
import math
import jax
import jax.numpy as jnp
from jax import lax

MODEL_DIMENSION = 1024
QUERY_HEADS = 8
KEY_VALUE_HEADS = 2
HEAD_DIMENSION = 64
MH = 24
MP = 64
NS = 128
KC = 4
FF = 2048
SEQUENCE_LENGTH = 1024
SPAN = 128
BATCH = 16


def levels(own_key, dims, cuts, low, largest):
    factor_of, own = 1.0, jax.random.fold_in(own_key, 6)
    for dim, parts in cuts:
        heights = jnp.exp(jax.random.uniform(jax.random.fold_in(own, dim), (parts,), jnp.float32, low / len(cuts), largest / len(cuts)))
        factor_of = factor_of * jnp.repeat(heights, dims[dim] // parts).reshape([-1 if axis == dim else 1 for axis in range(len(dims))])
    return factor_of


def centred(own_key, shape, spread, reach, cuts=(), kind=jnp.bfloat16):
    factor_of = levels(own_key, shape, cuts, -0.22, 0.18) if cuts else 1.0
    values = jax.random.normal(own_key, shape, jnp.float32) * spread * factor_of
    return jnp.minimum(jnp.maximum(values, -reach), reach).astype(kind)


def setup_inputs(seed: int = 0) -> dict:
    streams_of = jax.random.split(jax.random.key(seed), 19)
    return {
        "tokens": centred(streams_of[0], (BATCH, SEQUENCE_LENGTH, MODEL_DIMENSION), 1.0, 6.0, ((0, 8), (1, 2))),
        "out_grad": centred(streams_of[1], (BATCH, SEQUENCE_LENGTH, MODEL_DIMENSION), 1.0, 6.0, ((0, 8), (1, 2))),
        "norm_gains": jnp.clip(1.0 + 0.1 * jax.random.normal(streams_of[2], (2, MODEL_DIMENSION), jnp.float32), 0.5, 1.5).astype(jnp.bfloat16),
        "query_weight": centred(streams_of[3], (MODEL_DIMENSION, QUERY_HEADS * HEAD_DIMENSION), (MODEL_DIMENSION // 2) ** -0.5, 0.25, ((0, 16), (1, 2))),
        "key_value_matrix": centred(streams_of[4], (MODEL_DIMENSION, KEY_VALUE_HEADS, 2 * HEAD_DIMENSION), MODEL_DIMENSION ** -0.5, 0.1875, ((0, 16), (1, 2))),
        "output_weight": centred(streams_of[5], (QUERY_HEADS * HEAD_DIMENSION, MODEL_DIMENSION), (QUERY_HEADS * HEAD_DIMENSION // 8) ** -0.5, 0.75, ((0, 2), (1, 16))),
        "mixer_weight": centred(streams_of[6], (MODEL_DIMENSION, MH, 2 * MP), MODEL_DIMENSION ** -0.5, 0.1875, ((0, 16), (1, 2))),
        "state_weight": centred(streams_of[7], (MODEL_DIMENSION, 2 * NS), MODEL_DIMENSION ** -0.5, 0.1875, ((0, 16),)),
        "step_weight": centred(streams_of[8], (MODEL_DIMENSION, MH), MODEL_DIMENSION ** -0.5, 0.1875, ((0, 16), (1, 2))),
        "conv_inner": centred(streams_of[9], (KC + 1, MH * MP), 0.5, 2.5, ((1, 2),)),
        "conv_state": centred(streams_of[10], (KC + 1, 2 * NS), 0.5, 2.5),
        "step_bias": jnp.clip(-4.5 + 1.5 * jax.random.uniform(streams_of[11], (MH,), jnp.float32) ** levels(streams_of[11], (MH,), ((0, 2),), -0.2, 0.2), -4.5, -3.0).astype(jnp.bfloat16),
        "decay_log": jnp.clip(-2.5 + 3.5 * jax.random.uniform(streams_of[12], (MH,), jnp.float32) ** levels(streams_of[12], (MH,), ((0, 2),), -0.2, 0.2), -2.5, 1.0).astype(jnp.bfloat16),
        "skip_scale": jnp.clip(0.5 + 1.0 * jax.random.uniform(streams_of[13], (MH,), jnp.float32) ** levels(streams_of[13], (MH,), ((0, 2),), -0.2, 0.2), 0.5, 1.5).astype(jnp.bfloat16),
        "gated_gain": jnp.clip(1.0 + 0.1 * jax.random.normal(streams_of[14], (MH * MP,), jnp.float32), 0.5, 1.5).astype(jnp.bfloat16),
        "mamba_weight": centred(streams_of[15], (MH * MP, MODEL_DIMENSION), (MH * MP) ** -0.5, 0.15625, ((0, 2), (1, 16))),
        "gateup_weight": centred(streams_of[16], (MODEL_DIMENSION, 2, FF), MODEL_DIMENSION ** -0.5, 0.1875, ((0, 16), (2, 2))),
        "down_weight": centred(streams_of[17], (FF, MODEL_DIMENSION), FF ** -0.5, 0.125, ((0, 2), (1, 16))),
    }


EPSILON = 1e-05
HIGHEST = lax.Precision.HIGHEST
MASKED = -1e+30
ROPE_BASE = 10000.0

@jax.custom_vjp
def low(v):
    return lax.optimization_barrier(v.astype(jnp.bfloat16)).astype(jnp.float32)

@jax.custom_vjp
def low_back(v):
    return v

def low_keep(v):
    return (low(v), None)

def low_pass(kept, grad):
    return (grad,)

def back_keep(v):
    return (v, None)

def back_low(kept, grad):
    return (low(grad),)
low.defvjp(low_keep, low_pass)
low_back.defvjp(back_keep, back_low)

def rms_inverse(values):
    return lax.rsqrt(lax.optimization_barrier(jnp.mean(values * values, axis=-1, keepdims=True)) + EPSILON)

def rope_tables(first_place, place_count, head_width):
    position = (first_place + jnp.arange(place_count)).astype(jnp.float32)
    frequency = ROPE_BASE ** (-(jnp.arange(head_width // 2).astype(jnp.float32) * 2.0 / head_width))
    angles = position[:, None] * frequency[None, :]
    return (jnp.cos(angles), jnp.sin(angles))

def rotate(values, cosines, sines):
    half_width = values.shape[-1] // 2
    front = values[..., :half_width]
    behind = values[..., half_width:]
    return jnp.concatenate([front * cosines - behind * sines, behind * cosines + front * sines], axis=-1)

def conv_silu(padded, conv_table):
    tap_count = conv_table.shape[0] - 1
    length_out = padded.shape[1] - tap_count + 1
    summed = conv_table[tap_count]
    for tap_index in range(tap_count):
        summed = summed + conv_table[tap_index] * padded[:, tap_index:tap_index + length_out]
    return jax.nn.silu(summed)

def block_step(carry_state, pieces):
    block_x, block_write, block_read, block_size, block_rate = pieces
    block_len = block_x.shape[1]
    cumulative = jnp.cumsum(block_rate, axis=1)
    lower_mask = jnp.arange(block_len)[:, None] >= jnp.arange(block_len)[None, :]
    log_decay = jnp.where(lower_mask[None, :, :, None], cumulative[:, :, None, :] - cumulative[:, None, :, :], MASKED)
    intersection = jnp.einsum('gtn,gsn->gts', block_read, block_write, precision=HIGHEST)
    mixing = intersection[..., None] * jnp.exp(log_decay) * block_size[:, None, :, :]
    inside = jnp.einsum('gtsh,gshp->gthp', mixing, block_x, precision=HIGHEST)
    carried = jnp.einsum('gtn,ghpn->gthp', block_read, carry_state, precision=HIGHEST) * jnp.exp(cumulative)[..., None]
    tail_decay = jnp.exp(cumulative[:, -1:, :] - cumulative) * block_size
    fresh_state = jnp.einsum('gsh,gshp,gsn->ghpn', tail_decay, block_x, block_write, precision=HIGHEST)
    updated = carry_state * jnp.exp(cumulative[:, -1])[:, :, None, None] + fresh_state
    return (updated, inside + carried)

def state_space(head_x, write_vec, read_vec, step_size, decay_rate):
    head_group = head_x.shape[0]
    block_count = SEQUENCE_LENGTH // SPAN

    def to_blocks(values):
        return jnp.moveaxis(values.reshape((head_group, block_count, SPAN) + values.shape[2:]), 1, 0)
    initial = jnp.zeros((head_group, MH, MP, NS), jnp.float32)
    stepper = jax.checkpoint(block_step)
    final_state, outputs = lax.scan(stepper, initial, (to_blocks(head_x), to_blocks(write_vec), to_blocks(read_vec), to_blocks(step_size), to_blocks(decay_rate)))
    return jnp.moveaxis(outputs, 0, 1).reshape(head_group, SEQUENCE_LENGTH, MH, MP)

def forward(resid, norm_gains, query_weight, key_value_matrix, output_weight, mixer_weight, state_weight, step_weight, conv_inner, conv_state, step_bias, decay_log, skip_scale, gated_gain, mamba_weight, gateup_weight, down_weight):
    head_group = resid.shape[0]
    cosines, sines = rope_tables(0, SEQUENCE_LENGTH, HEAD_DIMENSION)
    cos_grid = cosines[None, :, None, :]
    sin_grid = sines[None, :, None, :]
    normed_one = low(resid * rms_inverse(resid) * norm_gains[0])
    query_lin = low_back(jnp.einsum('gtd,de->gte', normed_one, query_weight, precision=HIGHEST)).reshape(head_group, SEQUENCE_LENGTH, QUERY_HEADS, HEAD_DIMENSION)
    rotated_query = low(rotate(query_lin, cos_grid, sin_grid))
    pair_lin = low_back(jnp.einsum('gtd,dhe->gthe', normed_one, key_value_matrix, precision=HIGHEST))
    key_rot = low(rotate(pair_lin[..., :HEAD_DIMENSION], cos_grid, sin_grid))
    value = low(pair_lin[..., HEAD_DIMENSION:])
    grouped_heads = rotated_query.reshape(head_group, SEQUENCE_LENGTH, KEY_VALUE_HEADS, QUERY_HEADS // KEY_VALUE_HEADS, HEAD_DIMENSION)
    logits = low_back(jnp.einsum('gtkrd,gskd->gkrts', grouped_heads, key_rot, precision=HIGHEST) * HEAD_DIMENSION ** (-0.5))
    visible = jnp.arange(SEQUENCE_LENGTH)[None, :] <= jnp.arange(SEQUENCE_LENGTH)[:, None]
    logits = jnp.where(visible, logits, MASKED)
    probs = low(jax.nn.softmax(logits, axis=-1))
    attended = jnp.einsum('gkrts,gskd->gtkrd', probs, value, precision=HIGHEST).reshape(head_group, SEQUENCE_LENGTH, QUERY_HEADS * HEAD_DIMENSION)
    attended = low(low_back(attended))
    mixer_lin = low_back(jnp.einsum('gtd,dhe->gthe', normed_one, mixer_weight, precision=HIGHEST))
    gate_z = mixer_lin[..., :MP].reshape(head_group, SEQUENCE_LENGTH, MH * MP)
    inner_in = low(mixer_lin[..., MP:].reshape(head_group, SEQUENCE_LENGTH, MH * MP))
    state_in = low(low_back(jnp.einsum('gtd,dn->gtn', normed_one, state_weight, precision=HIGHEST)))
    step_raw = low_back(jnp.einsum('gtd,dh->gth', normed_one, step_weight, precision=HIGHEST))
    inner_conv = conv_silu(jnp.pad(inner_in, ((0, 0), (KC - 1, 0), (0, 0))), conv_inner)
    state_conv = conv_silu(jnp.pad(state_in, ((0, 0), (KC - 1, 0), (0, 0))), conv_state)
    step_size = jax.nn.softplus(step_raw + step_bias)
    decay_rate = step_size * -jnp.exp(decay_log)
    head_x = inner_conv.reshape(head_group, SEQUENCE_LENGTH, MH, MP)
    scanned = state_space(head_x, state_conv[..., :NS], state_conv[..., NS:], step_size, decay_rate)
    gated = (scanned + skip_scale[:, None] * head_x).reshape(head_group, SEQUENCE_LENGTH, MH * MP) * jax.nn.silu(gate_z)
    gated_low = low(gated * rms_inverse(gated) * gated_gain)
    branch = low_back(jnp.einsum('gte,ed->gtd', attended, output_weight, precision=HIGHEST) + jnp.einsum('gte,ed->gtd', gated_low, mamba_weight, precision=HIGHEST))
    middle = resid + branch
    normed_two = low(middle * rms_inverse(middle) * norm_gains[1])
    gate_up = low_back(jnp.einsum('gtd,dkf->gtkf', normed_two, gateup_weight, precision=HIGHEST))
    act = low(jax.nn.silu(gate_up[..., 0, :]) * gate_up[..., 1, :])
    return middle + jnp.einsum('gtf,fd->gtd', act, down_weight, precision=HIGHEST)

def reference(tokens, out_grad, norm_gains, query_weight, key_value_matrix, output_weight, mixer_weight, state_weight, step_weight, conv_inner, conv_state, step_bias, decay_log, skip_scale, gated_gain, mamba_weight, gateup_weight, down_weight):
    params = tuple((param_item.astype(jnp.float32) for param_item in (norm_gains, query_weight, key_value_matrix, output_weight, mixer_weight, state_weight, step_weight, conv_inner, conv_state, step_bias, decay_log, skip_scale, gated_gain, mamba_weight, gateup_weight, down_weight)))
    group_size = math.gcd(BATCH, max(1, 4096 // SEQUENCE_LENGTH))
    group_count = BATCH // group_size
    inputs = tokens.astype(jnp.float32).reshape(group_count, group_size, SEQUENCE_LENGTH, MODEL_DIMENSION)
    cotangents = out_grad.astype(jnp.float32).reshape(group_count, group_size, SEQUENCE_LENGTH, MODEL_DIMENSION)

    def one_group(totals, pieces):
        block_in, block_cot = pieces
        result, pullback = jax.vjp(forward, block_in, *params)
        grads = pullback(block_cot)
        summed = tuple((total_item + grad_item for total_item, grad_item in zip(totals, grads[1:])))
        return (summed, (result.astype(jnp.bfloat16), grads[0]))
    initial = tuple((jnp.zeros(param_item.shape, jnp.float32) for param_item in params))
    totals, (results, input_grads) = lax.scan(one_group, initial, (inputs, cotangents))
    return (results.reshape(BATCH, SEQUENCE_LENGTH, MODEL_DIMENSION), input_grads.reshape(BATCH, SEQUENCE_LENGTH, MODEL_DIMENSION), totals[0], totals[1], totals[2], totals[3], totals[4], totals[5], totals[6], totals[7], totals[8], totals[9], totals[10], totals[11], totals[12], totals[13], totals[14], totals[15])
```

```python
import jax
import jax.numpy as jnp
from jax import lax
from jax.sharding import PartitionSpec as P

HEAD_DIMENSION = 64
MP = 64
NS = 128
SPAN = 128


EPSILON = 1e-05
HIGHEST = lax.Precision.HIGHEST
MASKED = -1e30
ROPE_BASE = 10000.0
WEIGHT_AXES = ("fsdp", "ctx")


def shift_along(block, axis, distance):
    devices = range(lax.axis_size(axis))
    route = [(i - distance, i) for i in devices if i - distance in devices]
    return lax.ppermute(block, axis, route)


def sum_over(value, axis):
    count = lax.axis_size(axis)
    if count & (count - 1):
        return lax.psum(value, axis)
    stride = 1
    while stride < count:
        other = lax.ppermute(value, axis, [(i, i ^ stride) for i in range(count)])
        value = value + other
        stride *= 2
    return value


def gather_ctx(block, dim):
    count = lax.axis_size("ctx")
    if count == 1:
        return block
    if count > 2:
        return lax.all_gather(block, "ctx", axis=dim, tiled=True)
    other = lax.ppermute(block, "ctx", [(0, 1), (1, 0)])
    first = lax.axis_index("ctx") == 0
    return jnp.concatenate(
        [jnp.where(first, block, other), jnp.where(first, other, block)], axis=dim
    )


def scatter_sum_ctx(whole, dim):
    count = lax.axis_size("ctx")
    if count == 1:
        return whole
    if count > 2:
        return lax.psum_scatter(whole, "ctx", scatter_dimension=dim, tiled=True)
    half = whole.shape[dim] // 2
    low = lax.slice_in_dim(whole, 0, half, axis=dim)
    high = lax.slice_in_dim(whole, half, 2 * half, axis=dim)
    first = lax.axis_index("ctx") == 0
    kept = jnp.where(first, low, high)
    sent = jnp.where(first, high, low)
    return kept + lax.ppermute(sent, "ctx", [(0, 1), (1, 0)])


def carry_over(decay, state, forward):
    count = lax.axis_size("ctx")
    if count <= 2:
        moved = shift_along(state.astype(jnp.bfloat16), "ctx", 1 if forward else -1)
        return moved.astype(jnp.float32)
    place = lax.axis_index("ctx")
    decays = lax.all_gather(decay.astype(jnp.bfloat16), "ctx").astype(jnp.float32)
    states = lax.all_gather(state.astype(jnp.bfloat16), "ctx").astype(jnp.float32)
    total = jnp.zeros_like(state)
    order = range(count) if forward else range(count - 1, -1, -1)
    for k in order:
        reached = k < place if forward else k > place
        new = decays[k][:, :, None, None] * total + states[k]
        total = jnp.where(reached, new, total)
    return total


def rms_inverse(values):
    return lax.rsqrt(jnp.mean(values * values, axis=-1, keepdims=True) + EPSILON)


def norm_back(values, inverse, gain_values, gradient):
    weighted = gradient * gain_values
    inner_sum = jnp.sum(weighted * values, axis=-1, keepdims=True) / values.shape[-1]
    return (
        inverse * weighted - values * inverse**3 * inner_sum,
        jnp.sum(gradient * values * inverse, axis=0),
    )


def rope_tables(first_place, place_count, head_width):
    position = (first_place + jnp.arange(place_count)).astype(jnp.float32)
    frequency = ROPE_BASE ** (-(jnp.arange(head_width // 2).astype(jnp.float32) * 2.0 / head_width))
    angles = position[:, None] * frequency[None, :]
    return (jnp.cos(angles), jnp.sin(angles))


def rotate(values, cosines, sines):
    half_width = values.shape[-1] // 2
    front = values[..., :half_width]
    behind = values[..., half_width:]
    return jnp.concatenate(
        [front * cosines - behind * sines, behind * cosines + front * sines], axis=-1
    )


def conv_silu(padded, conv_table):
    tap_count = conv_table.shape[0] - 1
    length_out = padded.shape[1] - tap_count + 1
    summed = conv_table[tap_count]
    for tap_index in range(tap_count):
        summed = summed + conv_table[tap_index] * padded[:, tap_index : tap_index + length_out]
    return jax.nn.silu(summed)


def running_sum(values):
    length = values.shape[1]
    ones = (jnp.arange(length)[:, None] >= jnp.arange(length)[None, :]).astype(jnp.float32)
    return jnp.einsum("ts,gsh->gth", ones, values, precision=HIGHEST)


def block_step(carry_state, pieces):
    block_x, block_write, block_read, block_size, block_rate = pieces
    block_len = block_x.shape[1]
    cumulative = running_sum(block_rate)
    lower_mask = jnp.arange(block_len)[:, None] >= jnp.arange(block_len)[None, :]
    log_decay = jnp.where(
        lower_mask[None, :, :, None], cumulative[:, :, None, :] - cumulative[:, None, :, :], MASKED
    )
    intersection = jnp.einsum("gtn,gsn->gts", block_read, block_write, precision=HIGHEST)
    mixing = intersection[..., None] * jnp.exp(log_decay) * block_size[:, None, :, :]
    inside = jnp.einsum("gtsh,gshp->gthp", mixing, block_x, precision=HIGHEST)
    carried = (
        jnp.einsum("gtn,ghpn->gthp", block_read, carry_state, precision=HIGHEST)
        * jnp.exp(cumulative)[..., None]
    )
    tail_decay = jnp.exp(cumulative[:, -1:, :] - cumulative) * block_size
    fresh_state = jnp.einsum(
        "gsh,gshp,gsn->ghpn", tail_decay, block_x, block_write, precision=HIGHEST
    )
    updated = carry_state * jnp.exp(cumulative[:, -1])[:, :, None, None] + fresh_state
    return (updated, inside + carried, cumulative)


def mamba_local(padded, conv_table, step_raw, bias_values, decay_values):
    conv_output = conv_silu(padded, conv_table)
    seq_count, row_count, channels = conv_output.shape
    head_count = step_raw.shape[-1]
    inner_width = channels - 2 * NS
    head_inputs = conv_output[..., :inner_width].reshape(
        seq_count, row_count, head_count, inner_width // head_count
    )
    write_vectors = conv_output[..., inner_width : inner_width + NS]
    read_vectors = conv_output[..., inner_width + NS :]
    step_size = jax.nn.softplus(step_raw + bias_values)
    decay_rate = step_size * -jnp.exp(decay_values)
    block_count = row_count // SPAN

    def to_blocks(values):
        return jnp.moveaxis(values.reshape((seq_count, block_count, SPAN) + values.shape[2:]), 1, 0)

    def from_blocks(values):
        return jnp.moveaxis(values, 0, 1).reshape((seq_count, row_count) + values.shape[3:])

    def advance(carry, pieces):
        carry_state, offset = carry
        updated, output, cumulative = block_step(carry_state, pieces)
        return ((updated, offset + cumulative[:, -1]), (output, cumulative + offset[:, None, :]))

    initial = (
        jnp.zeros((seq_count, head_count, inner_width // head_count, NS), jnp.float32),
        jnp.zeros((seq_count, head_count), jnp.float32),
    )
    (final_state, total_rate), (outputs, cumulatives) = lax.scan(
        advance,
        initial,
        (
            to_blocks(head_inputs),
            to_blocks(write_vectors),
            to_blocks(read_vectors),
            to_blocks(step_size),
            to_blocks(decay_rate),
        ),
    )
    return (
        from_blocks(outputs),
        head_inputs,
        read_vectors,
        from_blocks(cumulatives),
        final_state,
        jnp.exp(total_rate),
    )


def mamba_finish(local_out, head_inputs, read_vectors, cumulative, incoming, skip_values, gate_z):
    carried = (
        jnp.einsum("gtn,ghpn->gthp", read_vectors, incoming, precision=HIGHEST)
        * jnp.exp(cumulative)[..., None]
    )
    values = local_out + carried + skip_values[:, None] * head_inputs
    return values.reshape(gate_z.shape) * jax.nn.silu(gate_z)


def dot(a, b):
    return jnp.dot(a, b, preferred_element_type=jnp.float32)


def dot_t(a, b):
    return lax.dot_general(a, b, (((1,), (1,)), ((), ())), preferred_element_type=jnp.float32)


def t_dot(a, b):
    return lax.dot_general(a, b, (((0,), (0,)), ((), ())), preferred_element_type=jnp.float32)


def shards(
    tokens,
    out_grad,
    norm_gains,
    query_weight,
    key_value_matrix,
    output_weight,
    mixer_weight,
    state_weight,
    step_weight,
    conv_inner,
    conv_state,
    step_bias,
    decay_log,
    skip_scale,
    gated_gain,
    mamba_weight,
    gateup_weight,
    down_weight,
):
    seq_count, row_count, model_width = tokens.shape
    total_rows = seq_count * row_count
    context_index = lax.axis_index("ctx")
    tensor_index = lax.axis_index("tp")
    tensor_count = lax.axis_size("tp")
    key_length = row_count * lax.axis_size("ctx")
    query_width = query_weight.shape[1]
    query_heads = query_width // HEAD_DIMENSION
    state_heads = step_bias.shape[0]
    inner_width = state_heads * MP
    hidden = down_weight.shape[0]
    own_rows = query_weight.shape[0]
    score_scale = HEAD_DIMENSION ** (-0.5)

    c_state = inner_width
    c_gate = c_state + 2 * NS
    c_query = c_gate + inner_width
    c_pair = c_query + query_width
    c_step = c_pair + 2 * HEAD_DIMENSION
    c_gain = c_step + state_heads
    pad = -(c_gain + 2) % 128
    mixer_parts = jnp.swapaxes(mixer_weight.reshape(own_rows, state_heads, 2, MP), 1, 2).reshape(
        own_rows, 2, inner_width
    )
    first_pack = jnp.concatenate(
        [
            mixer_parts[:, 1],
            state_weight,
            mixer_parts[:, 0],
            query_weight,
            key_value_matrix.reshape(own_rows, -1),
            step_weight,
            norm_gains.T,
            jnp.zeros((own_rows, pad), jnp.bfloat16),
        ],
        axis=1,
    )
    second_pack = jnp.concatenate(
        [gateup_weight.reshape(own_rows, 2 * hidden), down_weight.T, mamba_weight.T, output_weight.T],
        axis=1,
    )
    first_all = lax.all_gather(first_pack, WEIGHT_AXES, axis=0, tiled=True)
    second_all = lax.all_gather(second_pack, WEIGHT_AXES, axis=0, tiled=True)
    gateup_all = second_all[:, : 2 * hidden]
    down_all = second_all[:, 2 * hidden : 3 * hidden]
    mix_all = second_all[:, 3 * hidden :]

    residual = tokens.astype(jnp.float32).reshape(total_rows, model_width)
    first_inverse = rms_inverse(residual)
    first_gain = first_all[:, c_gain].astype(jnp.float32)
    second_gain = first_all[:, c_gain + 1].astype(jnp.float32)
    normed_one = (residual * first_inverse * first_gain).astype(jnp.bfloat16)
    cosines, sines = rope_tables(context_index * row_count, row_count, HEAD_DIMENSION)
    cos_grid = cosines[None, :, None, :]
    sin_grid = sines[None, :, None, :]
    conv_in = dot(normed_one, first_all[:, :c_gate]).astype(jnp.bfloat16).reshape(
        seq_count, row_count, c_gate
    )
    gate_z = dot(normed_one, first_all[:, c_gate:c_query]).reshape(
        seq_count, row_count, inner_width
    )
    small_lin = dot(normed_one, first_all[:, c_query:])
    query_lin = small_lin[:, :query_width].reshape(
        seq_count, row_count, query_heads, HEAD_DIMENSION
    )
    rotated_query = rotate(query_lin, cos_grid, sin_grid).astype(jnp.bfloat16)
    pair_lin = small_lin[:, query_width : query_width + 2 * HEAD_DIMENSION].reshape(
        seq_count, row_count, 2 * HEAD_DIMENSION
    )
    step_raw = small_lin[:, c_step - c_query : c_gain - c_query].reshape(
        seq_count, row_count, state_heads
    )
    key_rot = rotate(pair_lin[:, :, None, :HEAD_DIMENSION], cos_grid, sin_grid)[:, :, 0, :].astype(
        jnp.bfloat16
    )
    local_pairs = jnp.concatenate(
        [key_rot, pair_lin[..., HEAD_DIMENSION:].astype(jnp.bfloat16)], axis=-1
    )
    all_pairs = gather_ctx(local_pairs, 1)
    rim_width = conv_inner.shape[0] - 2
    rim_rows = shift_along(conv_in[:, row_count - rim_width :], "ctx", 1)

    query_rows = jnp.transpose(rotated_query, (0, 2, 1, 3)).reshape(
        seq_count, query_heads * row_count, HEAD_DIMENSION
    )
    query_place = context_index * row_count + jnp.tile(jnp.arange(row_count), query_heads)
    visible = jnp.arange(key_length)[None, :] <= query_place[:, None]

    def attend(pieces):
        query_one, pair_one = pieces
        logits = dot_t(query_one, pair_one[:, :HEAD_DIMENSION]) * score_scale
        logits = jnp.where(visible, logits, MASKED)
        largest = jnp.max(logits, axis=-1, keepdims=True)
        log_total = largest + jnp.log(jnp.sum(jnp.exp(logits - largest), axis=-1, keepdims=True))
        prob_low = jnp.exp(logits - log_total).astype(jnp.bfloat16)
        return (dot(prob_low, pair_one[:, HEAD_DIMENSION:]), log_total[:, 0])

    attended_rows, log_totals = lax.map(attend, (query_rows, all_pairs))
    attended = (
        jnp.transpose(
            attended_rows.reshape(seq_count, query_heads, row_count, HEAD_DIMENSION), (0, 2, 1, 3)
        )
        .reshape(total_rows, query_width)
        .astype(jnp.bfloat16)
    )
    padded = jnp.concatenate([rim_rows, conv_in], axis=1).astype(jnp.float32)
    conv_table = jnp.concatenate([conv_inner, conv_state], axis=1).astype(jnp.float32)
    local_values, local_back = jax.vjp(
        mamba_local,
        padded,
        conv_table,
        step_raw,
        step_bias.astype(jnp.float32),
        decay_log.astype(jnp.float32),
    )
    local_out, head_inputs, read_vectors, cumulative, final_state, block_decay = local_values
    incoming = carry_over(block_decay, final_state, True)
    gated_values, finish_back = jax.vjp(
        mamba_finish,
        local_out,
        head_inputs,
        read_vectors,
        cumulative,
        incoming,
        skip_scale.astype(jnp.float32),
        gate_z,
    )
    gated = gated_values.reshape(total_rows, inner_width)
    gate_gain = gated_gain.astype(jnp.float32)
    square_sum = sum_over(jnp.sum(gated * gated, axis=-1), "tp")
    gate_inverse = lax.rsqrt(square_sum / (inner_width * tensor_count) + EPSILON)[:, None]
    gated_low = (gated * gate_inverse * gate_gain).astype(jnp.bfloat16)
    mixed = jnp.concatenate([gated_low, attended], axis=1)
    branch = sum_over(dot_t(mixed, mix_all), "tp")
    middle = residual + branch
    second_inverse = rms_inverse(middle)
    normed_two = (middle * second_inverse * second_gain).astype(jnp.bfloat16)
    gate_val = dot(normed_two, gateup_all[:, :hidden])
    up_val = dot(normed_two, gateup_all[:, hidden:])
    sigmoid_gate = jax.nn.sigmoid(gate_val)
    silu_gate = gate_val * sigmoid_gate
    act_low = (silu_gate * up_val).astype(jnp.bfloat16)
    share_width = model_width // tensor_count
    feed_part = dot_t(act_low, down_all).astype(jnp.bfloat16)
    if tensor_count == 2:
        start_own = tensor_index * share_width
        own_part = lax.dynamic_slice_in_dim(feed_part, start_own, share_width, 1)
        other_part = lax.dynamic_slice_in_dim(feed_part, share_width - start_own, share_width, 1)
        feed_share = own_part.astype(jnp.float32) + lax.ppermute(
            other_part, "tp", [(0, 1), (1, 0)]
        ).astype(jnp.float32)
    else:
        feed_share = lax.psum_scatter(feed_part, "tp", scatter_dimension=1, tiled=True).astype(
            jnp.float32
        )
    middle_share = lax.dynamic_slice_in_dim(middle, tensor_index * share_width, share_width, 1)
    out_block = (
        (middle_share + feed_share).astype(jnp.bfloat16).reshape(seq_count, row_count, share_width)
    )
    cotangent = out_grad.reshape(total_rows, model_width)
    act_grad = dot(cotangent, down_all)
    gate_grad = (act_grad * up_val * sigmoid_gate * (1.0 + gate_val * (1.0 - sigmoid_gate))).astype(
        jnp.bfloat16
    )
    up_grad = (act_grad * silu_gate).astype(jnp.bfloat16)
    both_grads = jnp.concatenate([gate_grad, up_grad], axis=1)
    normed_two_grad = sum_over(dot_t(both_grads, gateup_all), "tp")
    second_back, second_gain_grad = norm_back(middle, second_inverse, second_gain, normed_two_grad)
    middle_grad = cotangent.astype(jnp.float32) + second_back
    branch_grad = middle_grad.astype(jnp.bfloat16)
    second_grads = jnp.concatenate(
        [
            t_dot(normed_two, both_grads).astype(jnp.bfloat16),
            t_dot(cotangent, act_low).astype(jnp.bfloat16),
            t_dot(branch_grad, mixed).astype(jnp.bfloat16),
        ],
        axis=1,
    )
    second_total = lax.psum_scatter(second_grads, WEIGHT_AXES, scatter_dimension=0, tiled=True)

    mixed_grad = dot(branch_grad, mix_all)
    attended_grad = mixed_grad[:, inner_width:].astype(jnp.bfloat16)
    gated_low_grad = mixed_grad[:, :inner_width]
    attended_grad_rows = jnp.transpose(
        attended_grad.reshape(seq_count, row_count, query_heads, HEAD_DIMENSION), (0, 2, 1, 3)
    ).reshape(seq_count, query_heads * row_count, HEAD_DIMENSION)

    def attend_back(pieces):
        query_one, pair_one, total_one, grad_one = pieces
        key_one = pair_one[:, :HEAD_DIMENSION]
        value_one = pair_one[:, HEAD_DIMENSION:]
        logits = dot_t(query_one, key_one) * score_scale
        logits = jnp.where(visible, logits, MASKED)
        prob_full = jnp.exp(logits - total_one[:, None])
        prob_grad = dot_t(grad_one, value_one)
        row_inner = jnp.sum(prob_full * prob_grad, axis=-1, keepdims=True)
        logit_grad = (prob_full * (prob_grad - row_inner)).astype(jnp.bfloat16)
        query_part = dot(logit_grad, key_one) * score_scale
        key_part = t_dot(logit_grad, query_one) * score_scale
        value_part = t_dot(prob_full.astype(jnp.bfloat16), grad_one)
        return (query_part, jnp.concatenate([key_part, value_part], axis=-1))

    coupling = sum_over(jnp.sum(gated_low_grad * gate_gain * gated, axis=-1), "tp")[:, None]
    query_grad_rows, pair_grad_all = lax.map(
        attend_back, (query_rows, all_pairs, log_totals, attended_grad_rows)
    )
    pair_grad = scatter_sum_ctx(pair_grad_all.astype(jnp.bfloat16), 1).astype(jnp.float32)
    query_grad = jnp.transpose(
        query_grad_rows.reshape(seq_count, query_heads, row_count, HEAD_DIMENSION), (0, 2, 1, 3)
    )
    query_lin_grad = (
        rotate(query_grad, cos_grid, -sin_grid)
        .reshape(total_rows, query_width)
        .astype(jnp.bfloat16)
    )
    key_lin_grad = rotate(pair_grad[:, :, None, :HEAD_DIMENSION], cos_grid, -sin_grid)[:, :, 0, :]
    pair_lin_grad = (
        jnp.concatenate([key_lin_grad, pair_grad[..., HEAD_DIMENSION:]], axis=-1)
        .reshape(total_rows, 2 * HEAD_DIMENSION)
        .astype(jnp.bfloat16)
    )
    gated_gain_grad = jnp.sum(gated_low_grad * gated * gate_inverse, axis=0)
    gated_grad = gate_inverse * gate_gain * gated_low_grad - gated * gate_inverse**3 * coupling / (
        inner_width * tensor_count
    )
    local_grad, inputs_grad, read_grad, cumulative_grad, incoming_grad, skip_grad, gate_z_grad = (
        finish_back(gated_grad.reshape(seq_count, row_count, inner_width))
    )
    later_grad = carry_over(block_decay, incoming_grad, False)
    decay_grad = jnp.sum(later_grad * incoming, axis=(2, 3))
    padded_grad, table_grad, step_raw_grad, bias_grad, decay_log_grad = local_back(
        (local_grad, inputs_grad, read_grad, cumulative_grad, later_grad, decay_grad)
    )
    rim_grad = shift_along(padded_grad[:, :rim_width].astype(jnp.bfloat16), "ctx", -1).astype(
        jnp.float32
    )
    conv_grad = padded_grad[:, rim_width:] + jnp.pad(
        rim_grad, ((0, 0), (row_count - rim_width, 0), (0, 0))
    )
    first_grads = jnp.concatenate(
        [
            conv_grad.reshape(total_rows, c_gate).astype(jnp.bfloat16),
            gate_z_grad.reshape(total_rows, inner_width).astype(jnp.bfloat16),
            query_lin_grad,
            pair_lin_grad,
            step_raw_grad.reshape(total_rows, state_heads).astype(jnp.bfloat16),
            jnp.zeros((total_rows, 2 + pad), jnp.bfloat16),
        ],
        axis=1,
    )
    first_total = lax.psum_scatter(
        t_dot(normed_one, first_grads).astype(jnp.bfloat16),
        WEIGHT_AXES,
        scatter_dimension=0,
        tiled=True,
    )
    normed_one_grad = sum_over(dot_t(first_grads, first_all), "tp")
    first_back, first_gain_grad = norm_back(residual, first_inverse, first_gain, normed_one_grad)
    tokens_grad = (middle_grad + first_back).reshape(seq_count, row_count, model_width)

    state_table = sum_over(table_grad[:, inner_width:], "tp")
    flat = jnp.concatenate(
        [
            table_grad[:, :inner_width].reshape(-1),
            state_table.reshape(-1),
            gated_gain_grad,
            bias_grad,
            decay_log_grad,
            skip_grad,
            first_gain_grad,
            second_gain_grad,
        ]
    )
    flat_size = flat.shape[0]
    flat = jnp.pad(flat, (0, -flat_size % 1024)).reshape(-1, 128)
    for axis in WEIGHT_AXES:
        flat = sum_over(flat, axis)
    flat = flat.reshape(-1)
    tap_rows = conv_inner.shape[0]
    sizes = (
        tap_rows * inner_width,
        tap_rows * 2 * NS,
        inner_width,
        state_heads,
        state_heads,
        state_heads,
        model_width,
        model_width,
    )
    pieces, start = [], 0
    for size in sizes:
        pieces.append(flat[start : start + size])
        start += size
    conv_inner_total = pieces[0].reshape(tap_rows, inner_width)
    conv_state_total = pieces[1].reshape(tap_rows, 2 * NS)
    gated_total, bias_total, decay_total, skip_total = pieces[2:6]
    gain_start = (lax.axis_index("fsdp") * lax.axis_size("ctx") + context_index) * own_rows
    gain_total = lax.dynamic_slice_in_dim(jnp.stack(pieces[6:8]), gain_start, own_rows, 1)

    wide_one = first_total.astype(jnp.float32)
    wide_two = second_total.astype(jnp.float32)
    mixer_total = jnp.stack(
        [
            wide_one[:, c_gate:c_query].reshape(own_rows, state_heads, MP),
            wide_one[:, :inner_width].reshape(own_rows, state_heads, MP),
        ],
        axis=2,
    ).reshape(own_rows, state_heads, 2 * MP)
    state_weight_total = sum_over(wide_one[:, c_state:c_gate], "tp")
    return (
        out_block,
        tokens_grad,
        gain_total,
        wide_one[:, c_query:c_pair],
        wide_one[:, c_pair:c_step].reshape(own_rows, 1, 2 * HEAD_DIMENSION),
        wide_two[:, 3 * hidden + inner_width :].T,
        mixer_total,
        state_weight_total,
        wide_one[:, c_step:c_gain],
        conv_inner_total,
        conv_state_total,
        bias_total,
        decay_total,
        skip_total,
        gated_total,
        wide_two[:, 3 * hidden : 3 * hidden + inner_width].T,
        wide_two[:, : 2 * hidden].reshape(own_rows, 2, hidden),
        wide_two[:, 2 * hidden : 3 * hidden].T,
    )


def solution(mesh):
    in_specs = (
        P("fsdp", "ctx", None),
        P("fsdp", "ctx", None),
        P(None, ("fsdp", "ctx")),
        P(("fsdp", "ctx"), "tp"),
        P(("fsdp", "ctx"), "tp", None),
        P("tp", ("fsdp", "ctx")),
        P(("fsdp", "ctx"), "tp", None),
        P(("fsdp", "ctx"), None),
        P(("fsdp", "ctx"), "tp"),
        P(None, "tp"),
        P(),
        P("tp"),
        P("tp"),
        P("tp"),
        P("tp"),
        P("tp", ("fsdp", "ctx")),
        P(("fsdp", "ctx"), None, "tp"),
        P("tp", ("fsdp", "ctx")),
    )
    out_specs = (
        P("fsdp", "ctx", "tp"),
        P("fsdp", "ctx", None),
        P(None, ("fsdp", "ctx")),
        P(("fsdp", "ctx"), "tp"),
        P(("fsdp", "ctx"), "tp", None),
        P("tp", ("fsdp", "ctx")),
        P(("fsdp", "ctx"), "tp", None),
        P(("fsdp", "ctx"), None),
        P(("fsdp", "ctx"), "tp"),
        P(None, "tp"),
        P(),
        P("tp"),
        P("tp"),
        P("tp"),
        P("tp"),
        P("tp", ("fsdp", "ctx")),
        P(("fsdp", "ctx"), None, "tp"),
        P("tp", ("fsdp", "ctx")),
    )
    return jax.shard_map(shards, mesh=mesh, in_specs=in_specs, out_specs=out_specs, check_vma=False)
```

```python
import functools

import jax
import jax.numpy as jnp
from jax import lax
from jax.experimental import pallas as pl
from jax.experimental.pallas import tpu as pltpu
from jax.sharding import PartitionSpec as P

HEAD_DIMENSION = 64
MP = 64
NS = 128
SPAN = 128


EPSILON = 1e-05
HIGHEST = lax.Precision.HIGHEST
MASKED = -1e30
ROPE_BASE = 10000.0
WEIGHT_AXES = ("fsdp", "ctx")
VMEM_LIMIT = 48 * 1024 * 1024
TAPS = 4
EDGE = 16


def shift_along(block, axis, distance):
    devices = range(lax.axis_size(axis))
    route = [(i - distance, i) for i in devices if i - distance in devices]
    return lax.ppermute(block, axis, route)


def sum_over(value, axis):
    count = lax.axis_size(axis)
    if count & (count - 1):
        return lax.psum(value, axis)
    stride = 1
    while stride < count:
        other = lax.ppermute(value, axis, [(i, i ^ stride) for i in range(count)])
        value = value + other
        stride *= 2
    return value


def gather_ctx(block, dim):
    count = lax.axis_size("ctx")
    if count == 1:
        return block
    if count > 2:
        return lax.all_gather(block, "ctx", axis=dim, tiled=True)
    other = lax.ppermute(block, "ctx", [(0, 1), (1, 0)])
    first = lax.axis_index("ctx") == 0
    return jnp.concatenate(
        [jnp.where(first, block, other), jnp.where(first, other, block)], axis=dim
    )


def scatter_sum_ctx(whole, dim):
    count = lax.axis_size("ctx")
    if count == 1:
        return whole
    if count > 2:
        return lax.psum_scatter(whole, "ctx", scatter_dimension=dim, tiled=True)
    half = whole.shape[dim] // 2
    low = lax.slice_in_dim(whole, 0, half, axis=dim)
    high = lax.slice_in_dim(whole, half, 2 * half, axis=dim)
    first = lax.axis_index("ctx") == 0
    kept = jnp.where(first, low, high)
    sent = jnp.where(first, high, low)
    return kept + lax.ppermute(sent, "ctx", [(0, 1), (1, 0)])


def carry_over(total_rate, state, forward):
    count = lax.axis_size("ctx")
    if count <= 2:
        return shift_along(state, "ctx", 1 if forward else -1)
    place = lax.axis_index("ctx")
    heads = state.shape[2] // MP
    decay = jnp.exp(total_rate[:, :, :heads]).astype(jnp.bfloat16)
    decays = jnp.repeat(lax.all_gather(decay, "ctx").astype(jnp.float32), MP, axis=3)
    states = lax.all_gather(state, "ctx").astype(jnp.float32)
    total = jnp.zeros(state.shape, jnp.float32)
    order = range(count) if forward else range(count - 1, -1, -1)
    for k in order:
        reached = k < place if forward else k > place
        total = jnp.where(reached, decays[k] * total + states[k], total)
    return total.astype(jnp.bfloat16)


def torus_route(step):
    def index(z, x, y):
        return (z * 2 + x) * 2 + y

    return [
        (index(z, x, y), index(*step(z, x, y)))
        for z in range(4)
        for x in range(2)
        for y in range(2)
    ]


def across(value, name, hop=1):
    step = {
        "x": lambda z, x, y: (z, 1 - x, y),
        "y": lambda z, x, y: (z, x, 1 - y),
        "z": lambda z, x, y: ((z + hop) % 4, x, y),
    }[name]
    return lax.ppermute(value, WEIGHT_AXES, torus_route(step))


def is_torus():
    return lax.axis_size("fsdp") == 8 and lax.axis_size("ctx") == 2


def torus_place():
    fsdp = lax.axis_index("fsdp")
    return {"z": fsdp // 2, "x": fsdp % 2, "y": lax.axis_index("ctx")}


def gather_weights(shard, order):
    if not is_torus():
        return lax.all_gather(shard, WEIGHT_AXES, axis=0, tiled=True)
    place = torus_place()
    done = ""
    value = shard
    for name in order:
        spot = sum(1 for other in "zxy" if other in done and "zxy".index(other) < "zxy".index(name))
        if name == "z":
            parts = [value] + [across(value, "z", hop) for hop in (1, 2, 3)]
            gathered = jnp.zeros((4, *value.shape), value.dtype)
            for hop, part in enumerate(parts):
                gathered = lax.dynamic_update_index_in_dim(
                    gathered, part, (place["z"] - hop) % 4, 0
                )
            value = gathered
        else:
            other = across(value, name)
            low = place[name] == 0
            value = jnp.stack(
                [jnp.where(low, value, other), jnp.where(low, other, value)], axis=spot
            )
        done += name
    return value.reshape(-1, shard.shape[1])


def scatter_begin(whole):
    if not is_torus():
        return lax.psum_scatter(whole, WEIGHT_AXES, scatter_dimension=0, tiled=True), ""
    return whole.reshape(4, 2, 2, -1, whole.shape[1]), "zxy"


def scatter_stage(state, name):
    value, left = state
    if not left:
        return state
    place = torus_place()[name]
    dim = left.index(name)

    def part(at):
        return lax.dynamic_index_in_dim(value, at, dim, keepdims=False)

    total = part(place).astype(jnp.float32)
    if name == "z":
        for hop in (1, 2, 3):
            total = total + across(part((place + hop) % 4), "z", hop).astype(jnp.float32)
    else:
        total = total + across(part(1 - place), name).astype(jnp.float32)
    left = left.replace(name, "")
    return (total.astype(jnp.bfloat16) if left else total), left


def scatter_end(state):
    return state[0].astype(jnp.float32)


def scatter_weights(whole, order):
    state = scatter_begin(whole)
    for name in order:
        state = scatter_stage(state, name)
    return scatter_end(state)


def scatter_gain(values):
    if not is_torus():
        return lax.psum_scatter(values, WEIGHT_AXES, scatter_dimension=0, tiled=True)
    place = torus_place()
    value = values.reshape(4, 4, -1)

    def part(array, at):
        return lax.dynamic_index_in_dim(array, at, 0, keepdims=False)

    total = part(value, place["z"])
    for hop in (1, 2, 3):
        total = total + across(part(value, (place["z"] + hop) % 4), "z", hop)
    result = part(total, 2 * place["x"] + place["y"])
    for dx, dy in ((0, 1), (1, 0), (1, 1)):
        sent = part(total, 2 * (place["x"] ^ dx) + (place["y"] ^ dy))
        route = torus_route(lambda z, x, y: (z, x ^ dx, y ^ dy))
        result = result + lax.ppermute(sent, WEIGHT_AXES, route)
    return result


def tie(*values):
    return lax.optimization_barrier(values)


def rms_inverse(values):
    return lax.rsqrt(jnp.mean(values * values, axis=-1, keepdims=True) + EPSILON)


def norm_back(values, inverse, gain_values, gradient):
    weighted = gradient * gain_values
    inner_sum = jnp.sum(weighted * values, axis=-1, keepdims=True) / values.shape[-1]
    return (
        inverse * weighted - values * inverse**3 * inner_sum,
        jnp.sum(gradient * values * inverse, axis=0),
    )


def rope_tables(first_place, place_count, head_width):
    position = (first_place + jnp.arange(place_count)).astype(jnp.float32)
    frequency = ROPE_BASE ** (-(jnp.arange(head_width // 2).astype(jnp.float32) * 2.0 / head_width))
    angles = position[:, None] * frequency[None, :]
    return (jnp.cos(angles), jnp.sin(angles))


def rotate(values, cosines, sines):
    half_width = values.shape[-1] // 2
    front = values[..., :half_width]
    behind = values[..., half_width:]
    return jnp.concatenate(
        [front * cosines - behind * sines, behind * cosines + front * sines], axis=-1
    )


def dot(a, b):
    return jnp.dot(a, b, preferred_element_type=jnp.float32)


def dot_t(a, b):
    return lax.dot_general(a, b, (((1,), (1,)), ((), ())), preferred_element_type=jnp.float32)


def t_dot(a, b):
    return lax.dot_general(a, b, (((0,), (0,)), ((), ())), preferred_element_type=jnp.float32)


def tall(kernel, grid, in_specs, out_specs, out_shape, scratch, flops, moved, exps):
    return pl.pallas_call(
        kernel,
        grid=grid,
        in_specs=in_specs,
        out_specs=out_specs,
        out_shape=out_shape,
        scratch_shapes=scratch,
        compiler_params=pltpu.CompilerParams(
            dimension_semantics=("arbitrary",) * len(grid), vmem_limit_bytes=VMEM_LIMIT
        ),
        cost_estimate=pl.CostEstimate(flops=flops, bytes_accessed=moved, transcendentals=exps),
    )


def lower_ones(transposed=False):
    rows = lax.broadcasted_iota(jnp.int32, (SPAN, SPAN), 0)
    columns = lax.broadcasted_iota(jnp.int32, (SPAN, SPAN), 1)
    return rows <= columns if transposed else rows >= columns


def exact_dot(a, b):
    return jnp.dot(a, b, preferred_element_type=jnp.float32, precision=HIGHEST)


def split_dot(a, b):
    high = a.astype(jnp.bfloat16)
    rest = (a - high.astype(jnp.float32)).astype(jnp.bfloat16)
    return dot(high, b) + dot(rest, b)


def pair_lanes(columns, pair):
    rows = columns.shape[0]
    lane = lax.broadcasted_iota(jnp.int32, (rows, 2 * MP), 1)
    left = jnp.broadcast_to(columns[:, 2 * pair : 2 * pair + 1], (rows, 2 * MP))
    right = jnp.broadcast_to(columns[:, 2 * pair + 1 : 2 * pair + 2], (rows, 2 * MP))
    return jnp.where(lane < MP, left, right)


def head_lanes(columns, pairs):
    return jnp.concatenate([pair_lanes(columns, j) for j in range(pairs)], axis=1)


def stacked_pair(values):
    lane = lax.broadcasted_iota(jnp.int32, values.shape, 1)
    zero = jnp.zeros_like(values)
    return jnp.concatenate(
        [jnp.where(lane < MP, values, zero), jnp.where(lane < MP, zero, values)], axis=0
    )


def load_window(window, edge_ref, before_ref, block_ref, first):
    edge = jnp.where(first, edge_ref[0].astype(jnp.float32), before_ref[...].astype(jnp.float32))
    window[0:EDGE, :] = edge
    window[EDGE:, :] = block_ref[...].astype(jnp.float32)


def window_conv(window, taps, lanes):
    total = taps[TAPS : TAPS + 1, lanes]
    for k in range(TAPS):
        start = EDGE - TAPS + 1 + k
        total = total + taps[k : k + 1, lanes] * window[start : start + SPAN, lanes]
    return total


def step_values(raw, heads):
    argument = raw + heads[0:1, :]
    size = jnp.maximum(argument, 0.0) + jnp.log1p(jnp.exp(-jnp.abs(argument)))
    rate = size * heads[1:2, :]
    return size, exact_dot(lower_ones().astype(jnp.float32), rate), rate, argument


def state_kernel(pairs, last, edge_ref, before_ref, block_ref, raw_ref, taps, heads, state_out, total_out, window, state, total):
    block = pl.program_id(1)
    inner = pairs * 2 * MP

    @pl.when(block == 0)
    def _():
        state[...] = jnp.zeros_like(state)
        total[...] = jnp.zeros_like(total)

    load_window(window, edge_ref, before_ref, block_ref, block == 0)
    conv = window_conv(window, taps, slice(0, inner + NS))
    conv = conv * jax.nn.sigmoid(conv)
    size, running, _, _ = step_values(raw_ref[...], heads[...])
    final = running[SPAN - 1 : SPAN, :]
    weight = jnp.exp(final - running) * size
    weighted = (conv[:, :inner] * head_lanes(weight, pairs)).astype(jnp.bfloat16)
    write_t = conv[:, inner:].T.astype(jnp.bfloat16)
    state[...] = state[...] * head_lanes(jnp.exp(final), pairs) + dot(write_t, weighted)
    total[...] = total[...] + final

    @pl.when(block == last)
    def _():
        state_out[0] = state[...].astype(jnp.bfloat16)
        total_out[0] = total[...]


def forward_kernel(pairs, edge_ref, before_ref, block_ref, raw_ref, taps, heads, gate_ref, skip_ref, incoming_ref, y_out, gated_out, square_out, entering_out, leaving_out, window, state):
    block = pl.program_id(1)
    inner = pairs * 2 * MP

    @pl.when(block == 0)
    def _():
        state[...] = incoming_ref[0].astype(jnp.float32)

    load_window(window, edge_ref, before_ref, block_ref, block == 0)
    conv = window_conv(window, taps, slice(0, inner + 2 * NS))
    conv = conv * jax.nn.sigmoid(conv)
    head_x = conv[:, :inner]
    write = conv[:, inner : inner + NS]
    read_low = conv[:, inner + NS :].astype(jnp.bfloat16)
    write_low = write.astype(jnp.bfloat16)
    size, running, _, _ = step_values(raw_ref[...], heads[...])
    running_t = running.T
    final = running[SPAN - 1 : SPAN, :]
    mask = lower_ones()
    product = dot_t(read_low, write_low)
    entering = state[...].astype(jnp.bfloat16)
    entering_out[0, 0] = entering
    carried = dot(read_low, entering) * head_lanes(jnp.exp(running), pairs)
    stepped = head_x * head_lanes(size, pairs)
    stepped_low = stepped.astype(jnp.bfloat16)
    inside = []
    for pair in range(pairs):
        mixing = []
        for head in (2 * pair, 2 * pair + 1):
            gap = running[:, head : head + 1] - running_t[head : head + 1, :]
            mixing.append((product * jnp.exp(jnp.where(mask, gap, MASKED))).astype(jnp.bfloat16))
        lanes = slice(pair * 2 * MP, (pair + 1) * 2 * MP)
        inside.append(dot(jnp.concatenate(mixing, axis=1), stacked_pair(stepped_low[:, lanes])))
    y = jnp.concatenate(inside, axis=1) + carried + skip_ref[0:1, :] * head_x
    gate = gate_ref[...]
    gated = y * (gate * jax.nn.sigmoid(gate))
    y_out[...] = y
    gated_out[...] = gated
    square_out[...] = jnp.sum(gated * gated, axis=1, keepdims=True)
    weighted = (stepped * head_lanes(jnp.exp(final - running), pairs)).astype(jnp.bfloat16)
    state[...] = state[...] * head_lanes(jnp.exp(final), pairs) + dot(
        write.T.astype(jnp.bfloat16), weighted
    )
    leaving_out[0, 0] = state[...].astype(jnp.bfloat16)


def gate_back_kernel(pairs, channels, last, edge_ref, before_ref, block_ref, raw_ref, taps, heads, gate_ref, y_ref, low_grad_ref, inverse_ref, coupling_ref, gain_ref, gate_grad_out, y_grad_out, gain_out, state_grad_out, window, state_grad, total):
    block = pl.program_id(1)
    first_of_all = (block == 0) & (pl.program_id(0) == 0)
    inner = pairs * 2 * MP

    @pl.when(block == 0)
    def _():
        state_grad[...] = jnp.zeros_like(state_grad)
        total[...] = jnp.zeros_like(total)

    @pl.when(first_of_all)
    def _():
        gain_out[...] = jnp.zeros_like(gain_out)

    gate = gate_ref[...]
    y = y_ref[...]
    low_grad = low_grad_ref[...]
    inverse = inverse_ref[...]
    sigmoid = jax.nn.sigmoid(gate)
    silu = gate * sigmoid
    gated = y * silu
    normed = gated * inverse
    gain_out[0:1, :] += jnp.sum(low_grad * normed, axis=0, keepdims=True)
    gated_grad = inverse * (
        gain_ref[0:1, :] * low_grad - normed * (inverse * coupling_ref[...] / channels)
    )
    y_grad = (gated_grad * silu).astype(jnp.bfloat16)
    y_grad_out[...] = y_grad
    gate_grad_out[...] = (gated_grad * y * (sigmoid * (1.0 + gate * (1.0 - sigmoid)))).astype(
        jnp.bfloat16
    )
    lanes = slice(inner + NS, inner + 2 * NS)
    load_window(window, edge_ref, before_ref, block_ref, block == 0)
    read = window_conv(window, taps, lanes)
    read = read * jax.nn.sigmoid(read)
    _, running, _, _ = step_values(raw_ref[...], heads[...])
    scaled = (
        y_grad.astype(jnp.float32) * head_lanes(jnp.exp(total[...] + running), pairs)
    ).astype(jnp.bfloat16)
    state_grad[...] += dot(read.T.astype(jnp.bfloat16), scaled)
    total[...] = total[...] + running[SPAN - 1 : SPAN, :]

    @pl.when(block == last)
    def _():
        state_grad_out[0] = state_grad[...].astype(jnp.bfloat16)


def backward_kernel(pairs, last, edge_ref, before_ref, block_ref, raw_ref, taps, heads, skip_ref, later_ref, entering_ref, leaving_ref, y_ref, y_grad_ref, conv_grad_out, step_grad_out, front_out, taps_out, heads_out, skip_out, window, state_grad, slopes):
    block = last - pl.program_id(1)
    first_step = pl.program_id(1) == 0
    inner = pairs * 2 * MP

    @pl.when(first_step)
    def _():
        state_grad[...] = later_ref[0].astype(jnp.float32)
        slopes[SPAN:, :] = jnp.zeros((8, slopes.shape[1]), jnp.float32)

    @pl.when(first_step & (pl.program_id(0) == 0))
    def _():
        taps_out[...] = jnp.zeros_like(taps_out)
        heads_out[...] = jnp.zeros_like(heads_out)
        skip_out[...] = jnp.zeros_like(skip_out)

    load_window(window, edge_ref, before_ref, block_ref, block == 0)
    before_silu = window_conv(window, taps, slice(0, inner + 2 * NS))
    sigmoid = jax.nn.sigmoid(before_silu)
    conv = before_silu * sigmoid
    head_x = conv[:, :inner]
    write = conv[:, inner : inner + NS]
    read = conv[:, inner + NS :]
    write_low = write.astype(jnp.bfloat16)
    read_low = read.astype(jnp.bfloat16)
    size, running, rate, argument = step_values(raw_ref[...], heads[...])
    running_t = running.T
    final = running[SPAN - 1 : SPAN, :]
    mask = lower_ones()
    mask_t = lower_ones(True)
    product = dot_t(read_low, write_low)
    product_t = dot_t(write_low, read_low)
    grad_low = y_grad_ref[...]
    grad = grad_low.astype(jnp.float32)
    entering = entering_ref[0, 0]
    state_low = state_grad[...].astype(jnp.bfloat16)
    grown = head_lanes(jnp.exp(running), pairs)
    tail = head_lanes(jnp.exp(final - running), pairs)
    size_lanes = head_lanes(size, pairs)
    stepped = head_x * size_lanes
    stepped_low = stepped.astype(jnp.bfloat16)
    from_state = dot(write_low, state_low) * tail
    product_grad = jnp.zeros((SPAN, SPAN), jnp.float32)
    slope_parts = []
    lane = lax.broadcasted_iota(jnp.int32, (SPAN, 2 * MP), 1)
    for pair in range(pairs):
        lanes = slice(pair * 2 * MP, (pair + 1) * 2 * MP)
        pair_grad = grad_low[:, lanes]
        mixing_t = []
        for side in (0, 1):
            head = 2 * pair + side
            column = running[:, head : head + 1]
            row = running_t[head : head + 1, :]
            decay = jnp.exp(jnp.where(mask, column - row, MASKED))
            decay_t = jnp.exp(jnp.where(mask_t, row - column, MASKED))
            mixing_t.append((product_t * decay_t).astype(jnp.bfloat16))
            own = (lane < MP) if side == 0 else (lane >= MP)
            one_head = jnp.where(own, pair_grad, jnp.zeros_like(pair_grad))
            product_grad = product_grad + dot_t(one_head, stepped_low[:, lanes]) * decay
        slope_parts.append(dot(jnp.concatenate(mixing_t, axis=1), stacked_pair(pair_grad)))
    slope = jnp.concatenate(slope_parts, axis=1) + from_state
    skip = skip_ref[0:1, :]
    x_grad = size_lanes * slope + skip * grad
    skip_out[0:1, :] += jnp.sum(grad * head_x, axis=0, keepdims=True)
    owner = lax.broadcasted_iota(jnp.int32, (inner, SPAN), 0) // MP
    ones = (owner == lax.broadcasted_iota(jnp.int32, (inner, SPAN), 1)).astype(jnp.bfloat16)
    y_scan = y_ref[...] - skip * head_x
    running_grad = split_dot(grad * y_scan - stepped * slope, ones)
    size_direct = split_dot(head_x * slope, ones)
    at_end = jnp.sum(
        state_grad[...] * leaving_ref[0, 0].astype(jnp.float32), axis=0, keepdims=True
    )
    at_end = split_dot(jnp.broadcast_to(at_end, (8, inner)), ones)[0:1, :]
    rate_grad = exact_dot(mask_t.astype(jnp.float32), running_grad) + at_end
    size_grad = size_direct + rate_grad * heads[1:2, :]
    valid = lax.broadcasted_iota(jnp.int32, (SPAN, SPAN), 1) < 2 * pairs
    raw_grad = jnp.where(valid, size_grad * jax.nn.sigmoid(argument), 0.0)
    step_grad_out[...] = raw_grad.astype(jnp.bfloat16)
    heads_out[0:1, :] += jnp.sum(raw_grad, axis=0, keepdims=True)
    heads_out[1:2, :] += jnp.sum(rate_grad * rate, axis=0, keepdims=True)
    grown_grad = (grad * grown).astype(jnp.bfloat16)
    product_grad_low = product_grad.astype(jnp.bfloat16)
    read_grad = dot(product_grad_low, write_low) + dot_t(grown_grad, entering)
    write_grad = dot(product_grad.T.astype(jnp.bfloat16), read_low) + dot_t(
        (stepped * tail).astype(jnp.bfloat16), state_low
    )
    state_grad[...] = state_grad[...] * head_lanes(jnp.exp(final), pairs) + dot(
        read.T.astype(jnp.bfloat16), grown_grad
    )
    conv_slope = jnp.concatenate([x_grad, write_grad, read_grad], axis=1) * (
        sigmoid * (1.0 + before_silu * (1.0 - sigmoid))
    )
    slopes[0:SPAN, :] = conv_slope
    taps_out[TAPS : TAPS + 1, :] += jnp.sum(conv_slope, axis=0, keepdims=True)
    total = jnp.zeros_like(conv_slope)
    for k in range(TAPS):
        start = EDGE - TAPS + 1 + k
        taps_out[k : k + 1, :] += jnp.sum(
            conv_slope * window[start : start + SPAN, :], axis=0, keepdims=True
        )
        ahead = TAPS - 1 - k
        total = total + taps[k : k + 1, :] * slopes[ahead : ahead + SPAN, :]
    conv_grad_out[...] = total.astype(jnp.bfloat16)
    slopes[SPAN:, :] = conv_slope[0:8, :]

    @pl.when(block == 0)
    def _():
        front_out[0] = conv_slope[0:EDGE, :].astype(jnp.bfloat16)


class Mixer:
    def __init__(self, conv_in, edge, step_lin, taps, heads, skip, gate_z, seq_count, step_block):
        self.seqs = seq_count
        self.rows = conv_in.shape[0] // seq_count
        self.blocks = self.rows // SPAN
        self.inner = gate_z.shape[1]
        self.pairs = self.inner // (2 * MP)
        self.width = conv_in.shape[1]
        self.base = (edge, conv_in, conv_in, step_lin, taps, heads)
        self.step_block = step_block
        self.skip, self.gate_z = skip, gate_z
        self.grid = (seq_count, self.blocks)

    def where(self, reverse):
        blocks = self.blocks
        return (lambda g, b: blocks - 1 - b) if reverse else (lambda g, b: b)

    def base_specs(self, reverse=False):
        at, blocks, per = self.where(reverse), self.blocks, SPAN // EDGE
        width, column = self.width, self.step_block
        return [
            pl.BlockSpec((1, EDGE, width), lambda g, b: (g, 0, 0)),
            pl.BlockSpec(
                (EDGE, width), lambda g, b: (g * blocks * per + jnp.maximum(at(g, b) * per - 1, 0), 0)
            ),
            pl.BlockSpec((SPAN, width), lambda g, b: (g * blocks + at(g, b), 0)),
            pl.BlockSpec((SPAN, SPAN), lambda g, b: (g * blocks + at(g, b), column)),
            pl.BlockSpec((8, width), lambda g, b: (0, 0)),
            pl.BlockSpec((8, SPAN), lambda g, b: (0, 0)),
        ]

    def rows_spec(self, width, reverse=False, dtype=None):
        at, blocks = self.where(reverse), self.blocks
        return pl.BlockSpec((SPAN, width), lambda g, b: (g * blocks + at(g, b), 0))

    def const_spec(self, width, rows=8):
        return pl.BlockSpec((rows, width), lambda g, b: (0, 0))

    def seq_spec(self, rows, width):
        return pl.BlockSpec((1, rows, width), lambda g, b: (g, 0, 0))

    def cost(self, products, arrays):
        count = self.seqs * self.blocks
        return (
            2 * count * products * SPAN * SPAN * self.inner,
            arrays * self.seqs * self.rows * self.inner,
            count * 2 * self.pairs * SPAN * SPAN,
        )

    def shape(self, width, dtype):
        return jax.ShapeDtypeStruct((self.seqs * self.rows, width), dtype)

    def window(self):
        return pltpu.VMEM((SPAN + EDGE, self.width), jnp.float32)

    def states(self):
        inner, last = self.inner, self.blocks - 1
        return tall(
            functools.partial(state_kernel, self.pairs, last),
            self.grid,
            self.base_specs(),
            [self.seq_spec(NS, inner), self.seq_spec(1, SPAN)],
            [
                jax.ShapeDtypeStruct((self.seqs, NS, inner), jnp.bfloat16),
                jax.ShapeDtypeStruct((self.seqs, 1, SPAN), jnp.float32),
            ],
            [self.window(), pltpu.VMEM((NS, inner), jnp.float32), pltpu.VMEM((1, SPAN), jnp.float32)],
            *self.cost(1, 3),
        )(*self.base)

    def forward(self, incoming):
        inner, blocks = self.inner, self.blocks
        rows = self.rows_spec
        saved = pl.BlockSpec((1, 1, NS, inner), lambda g, b: (g, b, 0, 0))
        return tall(
            functools.partial(forward_kernel, self.pairs),
            self.grid,
            [*self.base_specs(), rows(inner), self.const_spec(inner), self.seq_spec(NS, inner)],
            [rows(inner), rows(inner), rows(1), saved, saved],
            [
                self.shape(inner, jnp.float32),
                self.shape(inner, jnp.float32),
                self.shape(1, jnp.float32),
                jax.ShapeDtypeStruct((self.seqs, blocks, NS, inner), jnp.bfloat16),
                jax.ShapeDtypeStruct((self.seqs, blocks, NS, inner), jnp.bfloat16),
            ],
            [self.window(), pltpu.VMEM((NS, inner), jnp.float32)],
            *self.cost(4, 18),
        )(*self.base, self.gate_z, self.skip, incoming)

    def gate_back(self, y, low_grad, inverse, coupling, gain, channels):
        inner, last = self.inner, self.blocks - 1
        rows = self.rows_spec
        return tall(
            functools.partial(gate_back_kernel, self.pairs, channels, last),
            self.grid,
            [
                *self.base_specs(),
                *(rows(width) for width in (inner, inner, inner, 1, 1)),
                self.const_spec(inner),
            ],
            [rows(inner), rows(inner), self.const_spec(inner), self.seq_spec(NS, inner)],
            [
                self.shape(inner, jnp.bfloat16),
                self.shape(inner, jnp.bfloat16),
                jax.ShapeDtypeStruct((8, inner), jnp.float32),
                jax.ShapeDtypeStruct((self.seqs, NS, inner), jnp.bfloat16),
            ],
            [self.window(), pltpu.VMEM((NS, inner), jnp.float32), pltpu.VMEM((1, SPAN), jnp.float32)],
            *self.cost(1, 20),
        )(*self.base, self.gate_z, y, low_grad, inverse, coupling, gain)

    def backward(self, later, entering, leaving, y, y_grad):
        inner, width, last = self.inner, self.width, self.blocks - 1
        saved = pl.BlockSpec((1, 1, NS, inner), lambda g, b: (g, last - b, 0, 0))
        back = functools.partial(self.rows_spec, reverse=True)
        return tall(
            functools.partial(backward_kernel, self.pairs, last),
            self.grid,
            [
                *self.base_specs(True),
                self.const_spec(inner),
                self.seq_spec(NS, inner),
                saved,
                saved,
                back(inner),
                back(inner),
            ],
            [
                back(width),
                back(SPAN),
                self.seq_spec(EDGE, width),
                self.const_spec(width),
                self.const_spec(SPAN),
                self.const_spec(inner),
            ],
            [
                self.shape(width, jnp.bfloat16),
                self.shape(SPAN, jnp.bfloat16),
                jax.ShapeDtypeStruct((self.seqs, EDGE, width), jnp.bfloat16),
                jax.ShapeDtypeStruct((8, width), jnp.float32),
                jax.ShapeDtypeStruct((8, SPAN), jnp.float32),
                jax.ShapeDtypeStruct((8, inner), jnp.float32),
            ],
            [
                self.window(),
                pltpu.VMEM((NS, inner), jnp.float32),
                pltpu.VMEM((SPAN + 8, width), jnp.float32),
            ],
            *self.cost(9, 16),
        )(*self.base, self.skip, later, entering, leaving, y, y_grad)


def shards(
    tokens,
    out_grad,
    norm_gains,
    query_weight,
    key_value_matrix,
    output_weight,
    mixer_weight,
    state_weight,
    step_weight,
    conv_inner,
    conv_state,
    step_bias,
    decay_log,
    skip_scale,
    gated_gain,
    mamba_weight,
    gateup_weight,
    down_weight,
):
    seq_count, row_count, model_width = tokens.shape
    total_rows = seq_count * row_count
    context_index = lax.axis_index("ctx")
    tensor_index = lax.axis_index("tp")
    tensor_count = lax.axis_size("tp")
    key_length = row_count * lax.axis_size("ctx")
    query_width = query_weight.shape[1]
    query_heads = query_width // HEAD_DIMENSION
    state_heads = step_bias.shape[0]
    inner_width = state_heads * MP
    hidden = down_weight.shape[0]
    own_rows = query_weight.shape[0]
    score_scale = HEAD_DIMENSION ** (-0.5)

    c_state = inner_width
    c_gate = c_state + 2 * NS
    c_query = c_gate + inner_width
    c_pair = c_query + query_width
    c_step = c_pair + 2 * HEAD_DIMENSION
    c_gain = c_step + state_heads
    pad = -(c_gain + 2) % 128
    mixer_parts = jnp.swapaxes(mixer_weight.reshape(own_rows, state_heads, 2, MP), 1, 2).reshape(
        own_rows, 2, inner_width
    )
    pack_conv = jnp.concatenate([mixer_parts[:, 1], state_weight], axis=1)
    pack_small = jnp.concatenate(
        [
            query_weight,
            key_value_matrix.reshape(own_rows, -1),
            step_weight,
            norm_gains.T,
            jnp.zeros((own_rows, pad), jnp.bfloat16),
        ],
        axis=1,
    )
    second_pack = jnp.concatenate(
        [gateup_weight.reshape(own_rows, 2 * hidden), down_weight.T, mamba_weight.T, output_weight.T],
        axis=1,
    )
    small_all = gather_weights(pack_small, "xyz")
    conv_all = gather_weights(pack_conv, "zxy")
    gate_all = gather_weights(mixer_parts[:, 0], "yzx")
    second_pack, small_all, conv_all, gate_all = tie(second_pack, small_all, conv_all, gate_all)
    second_all = lax.all_gather(second_pack, WEIGHT_AXES, axis=0, tiled=True)
    gateup_all = second_all[:, : 2 * hidden]
    down_all = second_all[:, 2 * hidden : 3 * hidden]
    mix_all = second_all[:, 3 * hidden :]

    residual = tokens.astype(jnp.float32).reshape(total_rows, model_width)
    first_inverse = rms_inverse(residual)
    first_gain = small_all[:, c_gain - c_query].astype(jnp.float32)
    second_gain = small_all[:, c_gain + 1 - c_query].astype(jnp.float32)
    normed_one = (residual * first_inverse * first_gain).astype(jnp.bfloat16)
    cosines, sines = rope_tables(context_index * row_count, row_count, HEAD_DIMENSION)
    cos_grid = cosines[None, :, None, :]
    sin_grid = sines[None, :, None, :]
    conv_in = dot(normed_one, conv_all).astype(jnp.bfloat16)
    gate_z = dot(normed_one, gate_all)
    small_lin = dot(normed_one, small_all)
    query_lin = small_lin[:, :query_width].reshape(
        seq_count, row_count, query_heads, HEAD_DIMENSION
    )
    rotated_query = rotate(query_lin, cos_grid, sin_grid).astype(jnp.bfloat16)
    pair_lin = small_lin[:, query_width : query_width + 2 * HEAD_DIMENSION].reshape(
        seq_count, row_count, 2 * HEAD_DIMENSION
    )
    key_rot = rotate(pair_lin[:, :, None, :HEAD_DIMENSION], cos_grid, sin_grid)[:, :, 0, :].astype(
        jnp.bfloat16
    )
    local_pairs = jnp.concatenate(
        [key_rot, pair_lin[..., HEAD_DIMENSION:].astype(jnp.bfloat16)], axis=-1
    )
    all_pairs = gather_ctx(local_pairs, 1)
    conv_rows = conv_in.reshape(seq_count, row_count, c_gate)
    edge = shift_along(conv_rows[:, row_count - EDGE :], "ctx", 1)
    taps = jnp.pad(
        jnp.concatenate([conv_inner, conv_state], axis=1).astype(jnp.float32),
        ((0, 8 - conv_inner.shape[0]), (0, 0)),
    )
    head_rows = jnp.stack([step_bias.astype(jnp.float32), -jnp.exp(decay_log.astype(jnp.float32))])
    head_rows = jnp.pad(head_rows, ((0, 6), (0, SPAN - state_heads)))
    skip_rows = jnp.pad(jnp.repeat(skip_scale.astype(jnp.float32), MP)[None], ((0, 7), (0, 0)))
    mixer = Mixer(
        conv_in,
        edge,
        small_lin,
        taps,
        head_rows,
        skip_rows,
        gate_z,
        seq_count,
        (c_step - c_query) // SPAN,
    )
    final_state, total_rate = mixer.states()
    incoming = carry_over(total_rate, final_state, True)

    query_rows = jnp.transpose(rotated_query, (0, 2, 1, 3)).reshape(
        seq_count, query_heads * row_count, HEAD_DIMENSION
    )
    query_place = context_index * row_count + jnp.tile(jnp.arange(row_count), query_heads)
    visible = jnp.arange(key_length)[None, :] <= query_place[:, None]

    def attend(pieces):
        query_one, pair_one = pieces
        logits = dot_t(query_one, pair_one[:, :HEAD_DIMENSION]) * score_scale
        logits = jnp.where(visible, logits, MASKED)
        largest = jnp.max(logits, axis=-1, keepdims=True)
        log_total = largest + jnp.log(jnp.sum(jnp.exp(logits - largest), axis=-1, keepdims=True))
        prob_low = jnp.exp(logits - log_total).astype(jnp.bfloat16)
        return (dot(prob_low, pair_one[:, HEAD_DIMENSION:]), log_total[:, 0])

    attended_rows, log_totals = lax.map(attend, (query_rows, all_pairs))
    attended = (
        jnp.transpose(
            attended_rows.reshape(seq_count, query_heads, row_count, HEAD_DIMENSION), (0, 2, 1, 3)
        )
        .reshape(total_rows, query_width)
        .astype(jnp.bfloat16)
    )
    y_scan, gated, squares, entering, leaving = mixer.forward(incoming)
    gate_gain = gated_gain.astype(jnp.float32)
    square_sum = sum_over(squares, "tp")
    gate_inverse = lax.rsqrt(square_sum / (inner_width * tensor_count) + EPSILON)
    gated_low = (gated * gate_inverse * gate_gain).astype(jnp.bfloat16)
    mixed = jnp.concatenate([gated_low, attended], axis=1)
    branch = sum_over(dot_t(mixed, mix_all), "tp")
    middle = residual + branch
    second_inverse = rms_inverse(middle)
    normed_two = (middle * second_inverse * second_gain).astype(jnp.bfloat16)
    gate_val = dot(normed_two, gateup_all[:, :hidden])
    up_val = dot(normed_two, gateup_all[:, hidden:])
    sigmoid_gate = jax.nn.sigmoid(gate_val)
    silu_gate = gate_val * sigmoid_gate
    act_low = (silu_gate * up_val).astype(jnp.bfloat16)
    share_width = model_width // tensor_count
    feed_part = dot_t(act_low, down_all).astype(jnp.bfloat16)
    if tensor_count == 2:
        start_own = tensor_index * share_width
        own_part = lax.dynamic_slice_in_dim(feed_part, start_own, share_width, 1)
        other_part = lax.dynamic_slice_in_dim(feed_part, share_width - start_own, share_width, 1)
        feed_share = own_part.astype(jnp.float32) + lax.ppermute(
            other_part, "tp", [(0, 1), (1, 0)]
        ).astype(jnp.float32)
    else:
        feed_share = lax.psum_scatter(feed_part, "tp", scatter_dimension=1, tiled=True).astype(
            jnp.float32
        )
    middle_share = lax.dynamic_slice_in_dim(middle, tensor_index * share_width, share_width, 1)
    out_block = (
        (middle_share + feed_share).astype(jnp.bfloat16).reshape(seq_count, row_count, share_width)
    )
    cotangent = out_grad.reshape(total_rows, model_width)
    act_grad = dot(cotangent, down_all)
    gate_grad = (act_grad * up_val * sigmoid_gate * (1.0 + gate_val * (1.0 - sigmoid_gate))).astype(
        jnp.bfloat16
    )
    up_grad = (act_grad * silu_gate).astype(jnp.bfloat16)
    both_grads = jnp.concatenate([gate_grad, up_grad], axis=1)
    normed_two_grad = sum_over(dot_t(both_grads, gateup_all), "tp")
    second_back, second_gain_grad = norm_back(middle, second_inverse, second_gain, normed_two_grad)
    middle_grad = cotangent.astype(jnp.float32) + second_back
    branch_grad = middle_grad.astype(jnp.bfloat16)
    second_grads = jnp.concatenate(
        [
            t_dot(normed_two, both_grads).astype(jnp.bfloat16),
            t_dot(cotangent, act_low).astype(jnp.bfloat16),
            t_dot(branch_grad, mixed).astype(jnp.bfloat16),
        ],
        axis=1,
    )
    branch_grad, second_grads = lax.optimization_barrier((branch_grad, second_grads))
    second_total = lax.psum_scatter(second_grads, WEIGHT_AXES, scatter_dimension=0, tiled=True)

    attended_grad = dot(branch_grad, mix_all[:, inner_width:]).astype(jnp.bfloat16)
    gated_low_grad = dot(branch_grad, mix_all[:, :inner_width])
    attended_grad_rows = jnp.transpose(
        attended_grad.reshape(seq_count, row_count, query_heads, HEAD_DIMENSION), (0, 2, 1, 3)
    ).reshape(seq_count, query_heads * row_count, HEAD_DIMENSION)

    def attend_back(pieces):
        query_one, pair_one, total_one, grad_one = pieces
        key_one = pair_one[:, :HEAD_DIMENSION]
        value_one = pair_one[:, HEAD_DIMENSION:]
        logits = dot_t(query_one, key_one) * score_scale
        logits = jnp.where(visible, logits, MASKED)
        prob_full = jnp.exp(logits - total_one[:, None])
        prob_grad = dot_t(grad_one, value_one)
        row_inner = jnp.sum(prob_full * prob_grad, axis=-1, keepdims=True)
        logit_grad = (prob_full * (prob_grad - row_inner)).astype(jnp.bfloat16)
        query_part = dot(logit_grad, key_one) * score_scale
        key_part = t_dot(logit_grad, query_one) * score_scale
        value_part = t_dot(prob_full.astype(jnp.bfloat16), grad_one)
        return (query_part, jnp.concatenate([key_part, value_part], axis=-1))

    coupling = sum_over(
        jnp.sum(gated_low_grad * gate_gain * gated, axis=-1, keepdims=True), "tp"
    )
    gain_rows = jnp.pad(gate_gain[None], ((0, 7), (0, 0)))
    gate_z_grad, y_grad, gain_sums, incoming_grad = mixer.gate_back(
        y_scan, gated_low_grad, gate_inverse, coupling, gain_rows, inner_width * tensor_count
    )
    gated_gain_grad = gain_sums[0]
    later_grad = carry_over(total_rate, incoming_grad, False)
    query_grad_rows, pair_grad_all = lax.map(
        attend_back, (query_rows, all_pairs, log_totals, attended_grad_rows)
    )
    pair_grad = scatter_sum_ctx(pair_grad_all.astype(jnp.bfloat16), 1).astype(jnp.float32)
    query_grad = jnp.transpose(
        query_grad_rows.reshape(seq_count, query_heads, row_count, HEAD_DIMENSION), (0, 2, 1, 3)
    )
    query_lin_grad = (
        rotate(query_grad, cos_grid, -sin_grid)
        .reshape(total_rows, query_width)
        .astype(jnp.bfloat16)
    )
    key_lin_grad = rotate(pair_grad[:, :, None, :HEAD_DIMENSION], cos_grid, -sin_grid)[:, :, 0, :]
    pair_lin_grad = (
        jnp.concatenate([key_lin_grad, pair_grad[..., HEAD_DIMENSION:]], axis=-1)
        .reshape(total_rows, 2 * HEAD_DIMENSION)
        .astype(jnp.bfloat16)
    )
    early_grads = jnp.concatenate([gate_z_grad, query_lin_grad, pair_lin_grad], axis=1)
    early = t_dot(normed_one, early_grads).astype(jnp.bfloat16)
    early, y_grad = tie(early, y_grad)
    early = scatter_stage(scatter_begin(early), "y")
    conv_grad, step_grad, front_slopes, tap_sums, head_sums, skip_sums = mixer.backward(
        later_grad, entering, leaving, y_scan, y_grad
    )
    early_value, conv_grad = tie(early[0], conv_grad)
    early = scatter_stage((early_value, early[1]), "x")
    table_grad = tap_sums[: conv_inner.shape[0]]
    bias_grad = head_sums[0, :state_heads]
    decay_log_grad = head_sums[1, :state_heads]
    skip_grad = jnp.sum(skip_sums[0].reshape(state_heads, MP), axis=1)
    rim = TAPS - 1
    ahead = shift_along(front_slopes[:, :8], "ctx", -1).astype(jnp.float32)
    rim_grad = jnp.stack(
        [sum(taps[k] * ahead[:, i - k] for k in range(i + 1)) for i in range(rim)], axis=1
    )
    conv_grad = conv_grad.reshape(seq_count, row_count, c_gate)
    ending = conv_grad[:, row_count - rim :].astype(jnp.float32) + rim_grad
    conv_grad = lax.dynamic_update_slice_in_dim(
        conv_grad, ending.astype(jnp.bfloat16), row_count - rim, 1
    ).reshape(total_rows, c_gate)
    late_grads = jnp.concatenate([conv_grad, step_grad], axis=1)
    late = t_dot(normed_one, late_grads).astype(jnp.bfloat16)
    late_width = late.shape[1] // 2 // SPAN * SPAN
    late_one, late_two, late_grads = tie(late[:, :late_width], late[:, late_width:], late_grads)
    late_one = scatter_stage(scatter_begin(late_one), "y")
    late_two = scatter_stage(scatter_begin(late_two), "x")
    small_grads = jnp.concatenate([query_lin_grad, pair_lin_grad, step_grad], axis=1)
    normed_one_part = (
        dot_t(conv_grad, conv_all) + dot_t(gate_z_grad, gate_all) + dot_t(small_grads, small_all)
    )
    late_value, early_value, normed_one_part = tie(late_one[0], early[0], normed_one_part)
    late_one = scatter_stage((late_value, late_one[1]), "x")
    late_two = scatter_stage(late_two, "y")
    early = scatter_stage((early_value, early[1]), "z")
    normed_one_grad = sum_over(normed_one_part, "tp")
    late_total = jnp.concatenate(
        [scatter_end(scatter_stage(late_one, "z")), scatter_end(scatter_stage(late_two, "z"))], axis=1
    )
    early_total = scatter_end(early)
    first_back, first_gain_grad = norm_back(residual, first_inverse, first_gain, normed_one_grad)
    tokens_grad = (middle_grad + first_back).reshape(seq_count, row_count, model_width)

    state_table = sum_over(table_grad[:, inner_width:], "tp")
    flat = jnp.concatenate(
        [
            table_grad[:, :inner_width].reshape(-1),
            state_table.reshape(-1),
            gated_gain_grad,
            bias_grad,
            decay_log_grad,
            skip_grad,
        ]
    )
    flat_size = flat.shape[0]
    flat = jnp.pad(flat, (0, -flat_size % 1024)).reshape(-1, 128)
    for axis in WEIGHT_AXES:
        flat = sum_over(flat, axis)
    flat = flat.reshape(-1)
    tap_rows = conv_inner.shape[0]
    sizes = (
        tap_rows * inner_width,
        tap_rows * 2 * NS,
        inner_width,
        state_heads,
        state_heads,
        state_heads,
    )
    pieces, start = [], 0
    for size in sizes:
        pieces.append(flat[start : start + size])
        start += size
    conv_inner_total = pieces[0].reshape(tap_rows, inner_width)
    conv_state_total = pieces[1].reshape(tap_rows, 2 * NS)
    gated_total, bias_total, decay_total, skip_total = pieces[2:6]
    gain_total = jnp.stack([scatter_gain(first_gain_grad), scatter_gain(second_gain_grad)])

    wide_two = second_total.astype(jnp.float32)
    mixer_total = jnp.stack(
        [
            early_total[:, :inner_width].reshape(own_rows, state_heads, MP),
            late_total[:, :inner_width].reshape(own_rows, state_heads, MP),
        ],
        axis=2,
    ).reshape(own_rows, state_heads, 2 * MP)
    state_weight_total = sum_over(late_total[:, c_state:c_gate], "tp")
    return (
        out_block,
        tokens_grad,
        gain_total,
        early_total[:, inner_width : inner_width + query_width],
        early_total[:, inner_width + query_width :].reshape(own_rows, 1, 2 * HEAD_DIMENSION),
        wide_two[:, 3 * hidden + inner_width :].T,
        mixer_total,
        state_weight_total,
        late_total[:, c_gate : c_gate + state_heads],
        conv_inner_total,
        conv_state_total,
        bias_total,
        decay_total,
        skip_total,
        gated_total,
        wide_two[:, 3 * hidden : 3 * hidden + inner_width].T,
        wide_two[:, : 2 * hidden].reshape(own_rows, 2, hidden),
        wide_two[:, 2 * hidden : 3 * hidden].T,
    )


def solution(mesh):
    in_specs = (
        P("fsdp", "ctx", None),
        P("fsdp", "ctx", None),
        P(None, ("fsdp", "ctx")),
        P(("fsdp", "ctx"), "tp"),
        P(("fsdp", "ctx"), "tp", None),
        P("tp", ("fsdp", "ctx")),
        P(("fsdp", "ctx"), "tp", None),
        P(("fsdp", "ctx"), None),
        P(("fsdp", "ctx"), "tp"),
        P(None, "tp"),
        P(),
        P("tp"),
        P("tp"),
        P("tp"),
        P("tp"),
        P("tp", ("fsdp", "ctx")),
        P(("fsdp", "ctx"), None, "tp"),
        P("tp", ("fsdp", "ctx")),
    )
    out_specs = (
        P("fsdp", "ctx", "tp"),
        P("fsdp", "ctx", None),
        P(None, ("fsdp", "ctx")),
        P(("fsdp", "ctx"), "tp"),
        P(("fsdp", "ctx"), "tp", None),
        P("tp", ("fsdp", "ctx")),
        P(("fsdp", "ctx"), "tp", None),
        P(("fsdp", "ctx"), None),
        P(("fsdp", "ctx"), "tp"),
        P(None, "tp"),
        P(),
        P("tp"),
        P("tp"),
        P("tp"),
        P("tp"),
        P("tp", ("fsdp", "ctx")),
        P(("fsdp", "ctx"), None, "tp"),
        P("tp", ("fsdp", "ctx")),
    )
    return jax.shard_map(shards, mesh=mesh, in_specs=in_specs, out_specs=out_specs, check_vma=False)
```

```python
import functools

import jax
import jax.numpy as jnp
from jax import lax
from jax.experimental import pallas as pl
from jax.experimental.pallas import tpu as pltpu
from jax.sharding import PartitionSpec as P

HEAD_DIMENSION = 64
MP = 64
NS = 128
SPAN = 128


EPSILON = 1e-05
HIGHEST = lax.Precision.HIGHEST
MASKED = -1e30
ROPE_BASE = 10000.0
WEIGHT_AXES = ("fsdp", "ctx")
VMEM_LIMIT = 48 * 1024 * 1024
TAPS = 4
EDGE = 16


def shift_along(block, axis, distance):
    devices = range(lax.axis_size(axis))
    route = [(i - distance, i) for i in devices if i - distance in devices]
    return lax.ppermute(block, axis, route)


def sum_over(value, axis):
    count = lax.axis_size(axis)
    if count & (count - 1):
        return lax.psum(value, axis)
    stride = 1
    while stride < count:
        other = lax.ppermute(value, axis, [(i, i ^ stride) for i in range(count)])
        value = value + other
        stride *= 2
    return value


def gather_ctx(block, dim):
    count = lax.axis_size("ctx")
    if count == 1:
        return block
    if count > 2:
        return lax.all_gather(block, "ctx", axis=dim, tiled=True)
    other = lax.ppermute(block, "ctx", [(0, 1), (1, 0)])
    first = lax.axis_index("ctx") == 0
    return jnp.concatenate(
        [jnp.where(first, block, other), jnp.where(first, other, block)], axis=dim
    )


def scatter_sum_ctx(whole, dim):
    count = lax.axis_size("ctx")
    if count == 1:
        return whole
    if count > 2:
        return lax.psum_scatter(whole, "ctx", scatter_dimension=dim, tiled=True)
    half = whole.shape[dim] // 2
    low = lax.slice_in_dim(whole, 0, half, axis=dim)
    high = lax.slice_in_dim(whole, half, 2 * half, axis=dim)
    first = lax.axis_index("ctx") == 0
    kept = jnp.where(first, low, high)
    sent = jnp.where(first, high, low)
    return kept + lax.ppermute(sent, "ctx", [(0, 1), (1, 0)])


def carry_over(total_rate, state, forward):
    count = lax.axis_size("ctx")
    if count <= 2:
        return shift_along(state, "ctx", 1 if forward else -1)
    place = lax.axis_index("ctx")
    heads = state.shape[2] // MP
    decay = jnp.exp(total_rate[:, :, :heads]).astype(jnp.bfloat16)
    decays = jnp.repeat(lax.all_gather(decay, "ctx").astype(jnp.float32), MP, axis=3)
    states = lax.all_gather(state, "ctx").astype(jnp.float32)
    total = jnp.zeros(state.shape, jnp.float32)
    order = range(count) if forward else range(count - 1, -1, -1)
    for k in order:
        reached = k < place if forward else k > place
        total = jnp.where(reached, decays[k] * total + states[k], total)
    return total.astype(jnp.bfloat16)


def torus_route(step):
    def index(z, x, y):
        return (z * 2 + x) * 2 + y

    return [
        (index(z, x, y), index(*step(z, x, y)))
        for z in range(4)
        for x in range(2)
        for y in range(2)
    ]


def across(value, name, hop=1):
    step = {
        "x": lambda z, x, y: (z, 1 - x, y),
        "y": lambda z, x, y: (z, x, 1 - y),
        "z": lambda z, x, y: ((z + hop) % 4, x, y),
    }[name]
    return lax.ppermute(value, WEIGHT_AXES, torus_route(step))


def is_torus():
    return lax.axis_size("fsdp") == 8 and lax.axis_size("ctx") == 2


def torus_place():
    fsdp = lax.axis_index("fsdp")
    return {"z": fsdp // 2, "x": fsdp % 2, "y": lax.axis_index("ctx")}


def gather_weights(shard, order):
    if not is_torus():
        return lax.all_gather(shard, WEIGHT_AXES, axis=0, tiled=True), shard
    place = torus_place()
    done = ""
    value = shard
    early = None
    for name in order:
        spot = sum(1 for other in "zxy" if other in done and "zxy".index(other) < "zxy".index(name))
        if name == "z":
            parts = [value] + [across(value, "z", hop) for hop in (1, 2, 3)]
            gathered = jnp.zeros((4, *value.shape), value.dtype)
            for hop, part in enumerate(parts):
                gathered = lax.dynamic_update_index_in_dim(
                    gathered, part, (place["z"] - hop) % 4, 0
                )
            value = gathered
        else:
            other = across(value, name)
            low = place[name] == 0
            value = jnp.stack(
                [jnp.where(low, value, other), jnp.where(low, other, value)], axis=spot
            )
        done += name
        early = value if early is None else early
    return value.reshape(-1, shard.shape[1]), early


def scatter_begin(whole):
    if not is_torus():
        return lax.psum_scatter(whole, WEIGHT_AXES, scatter_dimension=0, tiled=True), ""
    return whole.reshape(4, 2, 2, -1, whole.shape[1]), "zxy"


def scatter_stage(state, name):
    value, left = state
    if not left:
        return state
    place = torus_place()[name]
    dim = left.index(name)

    def part(at):
        return lax.dynamic_index_in_dim(value, at, dim, keepdims=False)

    total = part(place).astype(jnp.float32)
    if name == "z":
        for hop in (1, 2, 3):
            total = total + across(part((place + hop) % 4), "z", hop).astype(jnp.float32)
    else:
        total = total + across(part(1 - place), name).astype(jnp.float32)
    left = left.replace(name, "")
    return (total.astype(jnp.bfloat16) if left else total), left


def scatter_end(state):
    return state[0].astype(jnp.float32)


def scatter_weights(whole, order):
    state = scatter_begin(whole)
    for name in order:
        state = scatter_stage(state, name)
    return scatter_end(state)


def scatter_gain(values):
    if not is_torus():
        return lax.psum_scatter(values, WEIGHT_AXES, scatter_dimension=0, tiled=True)
    place = torus_place()
    value = values.reshape(4, 4, -1)

    def part(array, at):
        return lax.dynamic_index_in_dim(array, at, 0, keepdims=False)

    total = part(value, place["z"])
    for hop in (1, 2, 3):
        total = total + across(part(value, (place["z"] + hop) % 4), "z", hop)
    result = part(total, 2 * place["x"] + place["y"])
    for dx, dy in ((0, 1), (1, 0), (1, 1)):
        sent = part(total, 2 * (place["x"] ^ dx) + (place["y"] ^ dy))
        route = torus_route(lambda z, x, y: (z, x ^ dx, y ^ dy))
        result = result + lax.ppermute(sent, WEIGHT_AXES, route)
    return result


def tie(*values):
    return lax.optimization_barrier(values)


def rms_inverse(values):
    return lax.rsqrt(jnp.mean(values * values, axis=-1, keepdims=True) + EPSILON)


def norm_back(values, inverse, gain_values, gradient):
    weighted = gradient * gain_values
    inner_sum = jnp.sum(weighted * values, axis=-1, keepdims=True) / values.shape[-1]
    return (
        inverse * weighted - values * inverse**3 * inner_sum,
        jnp.sum(gradient * values * inverse, axis=0),
    )


def rope_tables(first_place, place_count, head_width):
    position = (first_place + jnp.arange(place_count)).astype(jnp.float32)
    frequency = ROPE_BASE ** (-(jnp.arange(head_width // 2).astype(jnp.float32) * 2.0 / head_width))
    angles = position[:, None] * frequency[None, :]
    return (jnp.cos(angles), jnp.sin(angles))


def dot(a, b):
    return jnp.dot(a, b, preferred_element_type=jnp.float32)


def dot_t(a, b):
    return lax.dot_general(a, b, (((1,), (1,)), ((), ())), preferred_element_type=jnp.float32)


def t_dot(a, b):
    return lax.dot_general(a, b, (((0,), (0,)), ((), ())), preferred_element_type=jnp.float32)


def tall(kernel, grid, in_specs, out_specs, out_shape, scratch, flops, moved, exps):
    return pl.pallas_call(
        kernel,
        grid=grid,
        in_specs=in_specs,
        out_specs=out_specs,
        out_shape=out_shape,
        scratch_shapes=scratch,
        compiler_params=pltpu.CompilerParams(
            dimension_semantics=("arbitrary",) * len(grid), vmem_limit_bytes=VMEM_LIMIT
        ),
        cost_estimate=pl.CostEstimate(flops=flops, bytes_accessed=moved, transcendentals=exps),
    )


def turn(values, cosines, sines):
    rows, width = values.shape
    half = HEAD_DIMENSION // 2
    lane = lax.broadcasted_iota(jnp.int32, (rows, width), 1)
    swapped = jnp.where(
        lane % HEAD_DIMENSION < half, pltpu.roll(values, width - half, 1), pltpu.roll(values, half, 1)
    )
    times = width // cosines.shape[1]
    if times > 1:
        cosines = jnp.concatenate([cosines] * times, axis=1)
        sines = jnp.concatenate([sines] * times, axis=1)
    return values * cosines + swapped * sines


def turn_kernel(query_width, lin_ref, tables, query_out, pair_out):
    lin = lin_ref[...]
    query_out[...] = turn(lin[:, :query_width], tables[0], tables[1]).astype(jnp.bfloat16)
    pair_out[...] = turn(lin[:, query_width:], tables[2], tables[3]).astype(jnp.bfloat16)


def turn_back_kernel(grad_ref, tables, grad_out):
    grad = grad_ref[...].astype(jnp.float32)
    grad_out[...] = turn(grad, tables[2], -tables[3]).astype(jnp.bfloat16)


def one_head(tile_ref, head, to_left):
    start = head // 2 * 2 * HEAD_DIMENSION
    tile = tile_ref[:, start : start + 2 * HEAD_DIMENSION]
    is_left = head % 2 == 0
    if is_left != to_left:
        tile = pltpu.roll(tile.astype(jnp.float32), HEAD_DIMENSION, 1).astype(jnp.bfloat16)
    lane = lax.broadcasted_iota(jnp.int32, tile.shape, 1)
    kept = lane < HEAD_DIMENSION if to_left else lane >= HEAD_DIMENSION
    return jnp.where(kept, tile, jnp.zeros_like(tile))


def logits_t(pair, query, start, scale):
    logits = dot_t(pair, query) * scale
    key = lax.broadcasted_iota(jnp.int32, logits.shape, 0)
    place = lax.broadcasted_iota(jnp.int32, logits.shape, 1) + start
    return jnp.where(key <= place, logits, MASKED)


def join_heads(parts_t, on_left):
    tiles = []
    for left, right in zip(parts_t[::2], parts_t[1::2]):
        half = HEAD_DIMENSION
        pick = (lambda v: v[:half]) if on_left else (lambda v: v[half:])
        tiles.append(jnp.concatenate([pick(left), pick(right)], axis=0).T)
    return jnp.concatenate(tiles, axis=1)


def attend_kernel(heads, scale, start_ref, query_ref, pair_ref, out_ref, total_ref, pair_t):
    @pl.when(pl.program_id(1) == 0)
    def _():
        pair_t[...] = pair_ref[0].astype(jnp.float32).T.astype(jnp.bfloat16)

    pair = pair_ref[0]
    rows = query_ref.shape[0]
    start = start_ref[0] + pl.program_id(1) * rows
    outs = []
    for head in range(heads):
        logits = logits_t(pair, one_head(query_ref, head, True), start, scale)
        largest = jnp.max(logits, axis=0, keepdims=True)
        weights = jnp.exp(logits - largest)
        total = jnp.sum(weights, axis=0, keepdims=True)
        total_ref[0, head : head + 1, :] = largest + jnp.log(total)
        probs = (weights * (1.0 / total)).astype(jnp.bfloat16)
        outs.append(dot(pair_t[...], probs))
    out_ref[...] = join_heads(outs, False).astype(jnp.bfloat16)


def attend_back_kernel(heads, scale, last, start_ref, query_ref, pair_ref, total_ref, grad_ref, tables, query_out, pair_out, pair_t, pair_sum):
    @pl.when(pl.program_id(1) == 0)
    def _():
        pair_t[...] = pair_ref[0].astype(jnp.float32).T.astype(jnp.bfloat16)
        pair_sum[...] = jnp.zeros_like(pair_sum)

    pair = pair_ref[0]
    rows = query_ref.shape[0]
    start = start_ref[0] + pl.program_id(1) * rows
    outs = []
    for head in range(heads):
        query = one_head(query_ref, head, True)
        grad = one_head(grad_ref, head, False)
        probs = jnp.exp(
            logits_t(pair, query, start, scale) - total_ref[0, head : head + 1, :]
        )
        prob_grad = dot_t(pair, grad)
        inner_sum = jnp.sum(probs * prob_grad, axis=0, keepdims=True)
        logit_grad = (probs * (prob_grad - inner_sum)).astype(jnp.bfloat16)
        outs.append(dot(pair_t[...], logit_grad))
        pair_sum[...] += dot(logit_grad, query) * scale + dot(probs.astype(jnp.bfloat16), grad)
    query_grad = join_heads(outs, True) * scale
    query_out[...] = turn(query_grad, tables[0], -tables[1]).astype(jnp.bfloat16)

    @pl.when(pl.program_id(1) == last)
    def _():
        pair_out[0] = pair_sum[...].astype(jnp.bfloat16)


class Attention:
    def __init__(self, tables, start, seq_count, rows, keys, heads):
        self.tables, self.start = tables, start
        self.seqs, self.rows, self.keys, self.heads = seq_count, rows, keys, heads
        self.width = heads * HEAD_DIMENSION
        self.tile = min(256, rows)
        self.tiles = rows // self.tile
        self.scale = HEAD_DIMENSION ** (-0.5)

    def specs(self):
        tile, tiles, pair_width = self.tile, self.tiles, 2 * HEAD_DIMENSION
        return {
            "start": pl.BlockSpec(memory_space=pltpu.SMEM),
            "query": pl.BlockSpec((tile, self.width), lambda g, b: (g * tiles + b, 0)),
            "local": pl.BlockSpec((tile, pair_width), lambda g, b: (g * tiles + b, 0)),
            "lin": pl.BlockSpec((tile, self.width + pair_width), lambda g, b: (g * tiles + b, 0)),
            "pair": pl.BlockSpec((1, self.keys, pair_width), lambda g, b: (g, 0, 0)),
            "total": pl.BlockSpec((1, 8, tile), lambda g, b: (g, 0, b)),
            "tables": pl.BlockSpec((4, tile, 2 * HEAD_DIMENSION), lambda g, b: (0, b, 0)),
        }

    def call(self, kernel, ins, outs, shapes, scratch, products, operands):
        specs = self.specs()
        size = self.seqs * self.rows * self.keys * self.heads
        return tall(
            kernel,
            (self.seqs, self.tiles),
            [specs[name] for name in ins],
            [specs[name] for name in outs],
            shapes,
            scratch,
            2 * products * size * 2 * HEAD_DIMENSION,
            self.seqs * (self.rows + self.keys) * 1024,
            size if products else 0,
        )(*operands)

    def pair_shape(self):
        return jax.ShapeDtypeStruct((self.seqs * self.rows, 2 * HEAD_DIMENSION), jnp.bfloat16)

    def query_shape(self):
        return jax.ShapeDtypeStruct((self.seqs * self.rows, self.width), jnp.bfloat16)

    def prepare(self, lin):
        return self.call(
            functools.partial(turn_kernel, self.width),
            ("lin", "tables"),
            ("query", "local"),
            [self.query_shape(), self.pair_shape()],
            [],
            0,
            (lin, self.tables),
        )

    def forward(self, query, pairs):
        return self.call(
            functools.partial(attend_kernel, self.heads, self.scale),
            ("start", "query", "pair"),
            ("query", "total"),
            [self.query_shape(), jax.ShapeDtypeStruct((self.seqs, 8, self.rows), jnp.float32)],
            [pltpu.VMEM((2 * HEAD_DIMENSION, self.keys), jnp.bfloat16)],
            2,
            (self.start, query, pairs),
        )

    def backward(self, query, pairs, totals, grad):
        return self.call(
            functools.partial(attend_back_kernel, self.heads, self.scale, self.tiles - 1),
            ("start", "query", "pair", "total", "query", "tables"),
            ("query", "pair"),
            [
                self.query_shape(),
                jax.ShapeDtypeStruct((self.seqs, self.keys, 2 * HEAD_DIMENSION), jnp.bfloat16),
            ],
            [
                pltpu.VMEM((2 * HEAD_DIMENSION, self.keys), jnp.bfloat16),
                pltpu.VMEM((self.keys, 2 * HEAD_DIMENSION), jnp.float32),
            ],
            5,
            (self.start, query, pairs, totals, grad, self.tables),
        )

    def pair_back(self, grad):
        return self.call(
            turn_back_kernel,
            ("local", "tables"),
            ("local",),
            [self.pair_shape()],
            [],
            0,
            (grad, self.tables),
        )[0]


def lower_ones(transposed=False):
    rows = lax.broadcasted_iota(jnp.int32, (SPAN, SPAN), 0)
    columns = lax.broadcasted_iota(jnp.int32, (SPAN, SPAN), 1)
    return rows <= columns if transposed else rows >= columns


def exact_dot(a, b):
    return jnp.dot(a, b, preferred_element_type=jnp.float32, precision=HIGHEST)


def split_dot(a, b):
    high = a.astype(jnp.bfloat16)
    rest = (a - high.astype(jnp.float32)).astype(jnp.bfloat16)
    return dot(high, b) + dot(rest, b)


def pair_lanes(columns, pair):
    rows = columns.shape[0]
    lane = lax.broadcasted_iota(jnp.int32, (rows, 2 * MP), 1)
    left = jnp.broadcast_to(columns[:, 2 * pair : 2 * pair + 1], (rows, 2 * MP))
    right = jnp.broadcast_to(columns[:, 2 * pair + 1 : 2 * pair + 2], (rows, 2 * MP))
    return jnp.where(lane < MP, left, right)


def head_lanes(columns, pairs):
    return jnp.concatenate([pair_lanes(columns, j) for j in range(pairs)], axis=1)


def stacked_pair(values):
    lane = lax.broadcasted_iota(jnp.int32, values.shape, 1)
    zero = jnp.zeros_like(values)
    return jnp.concatenate(
        [jnp.where(lane < MP, values, zero), jnp.where(lane < MP, zero, values)], axis=0
    )


def load_window(window, edge_ref, before_ref, block_ref, first):
    edge = jnp.where(first, edge_ref[0].astype(jnp.float32), before_ref[...].astype(jnp.float32))
    window[0:EDGE, :] = edge
    window[EDGE:, :] = block_ref[...].astype(jnp.float32)


def window_conv(window, taps, lanes):
    total = taps[TAPS : TAPS + 1, lanes]
    for k in range(TAPS):
        start = EDGE - TAPS + 1 + k
        total = total + taps[k : k + 1, lanes] * window[start : start + SPAN, lanes]
    return total


def step_values(raw, heads):
    argument = raw + heads[0:1, :]
    size = jnp.maximum(argument, 0.0) + jnp.log1p(jnp.exp(-jnp.abs(argument)))
    rate = size * heads[1:2, :]
    return size, exact_dot(lower_ones().astype(jnp.float32), rate), rate, argument


def state_kernel(pairs, last, edge_ref, before_ref, block_ref, raw_ref, taps, heads, state_out, total_out, window, state, total):
    block = pl.program_id(1)
    inner = pairs * 2 * MP

    @pl.when(block == 0)
    def _():
        state[...] = jnp.zeros_like(state)
        total[...] = jnp.zeros_like(total)

    load_window(window, edge_ref, before_ref, block_ref, block == 0)
    conv = window_conv(window, taps, slice(0, inner + NS))
    conv = conv * jax.nn.sigmoid(conv)
    size, running, _, _ = step_values(raw_ref[...], heads[...])
    final = running[SPAN - 1 : SPAN, :]
    weight = jnp.exp(final - running) * size
    weighted = (conv[:, :inner] * head_lanes(weight, pairs)).astype(jnp.bfloat16)
    write_t = conv[:, inner:].T.astype(jnp.bfloat16)
    state[...] = state[...] * head_lanes(jnp.exp(final), pairs) + dot(write_t, weighted)
    total[...] = total[...] + final

    @pl.when(block == last)
    def _():
        state_out[0] = state[...].astype(jnp.bfloat16)
        total_out[0] = total[...]


def forward_kernel(pairs, edge_ref, before_ref, block_ref, raw_ref, taps, heads, gate_ref, skip_ref, incoming_ref, y_out, gated_out, square_out, entering_out, leaving_out, window, state):
    block = pl.program_id(1)
    inner = pairs * 2 * MP

    @pl.when(block == 0)
    def _():
        state[...] = incoming_ref[0].astype(jnp.float32)

    load_window(window, edge_ref, before_ref, block_ref, block == 0)
    conv = window_conv(window, taps, slice(0, inner + 2 * NS))
    conv = conv * jax.nn.sigmoid(conv)
    head_x = conv[:, :inner]
    write = conv[:, inner : inner + NS]
    read_low = conv[:, inner + NS :].astype(jnp.bfloat16)
    write_low = write.astype(jnp.bfloat16)
    size, running, _, _ = step_values(raw_ref[...], heads[...])
    running_t = running.T
    final = running[SPAN - 1 : SPAN, :]
    mask = lower_ones()
    product = dot_t(read_low, write_low)
    entering = state[...].astype(jnp.bfloat16)
    entering_out[0, 0] = entering
    carried = dot(read_low, entering) * head_lanes(jnp.exp(running), pairs)
    stepped = head_x * head_lanes(size, pairs)
    stepped_low = stepped.astype(jnp.bfloat16)
    inside = []
    for pair in range(pairs):
        mixing = []
        for head in (2 * pair, 2 * pair + 1):
            gap = running[:, head : head + 1] - running_t[head : head + 1, :]
            mixing.append((product * jnp.exp(jnp.where(mask, gap, MASKED))).astype(jnp.bfloat16))
        lanes = slice(pair * 2 * MP, (pair + 1) * 2 * MP)
        inside.append(dot(jnp.concatenate(mixing, axis=1), stacked_pair(stepped_low[:, lanes])))
    y = jnp.concatenate(inside, axis=1) + carried + skip_ref[0:1, :] * head_x
    gate = gate_ref[...]
    gated = y * (gate * jax.nn.sigmoid(gate))
    y_out[...] = y
    gated_out[...] = gated
    square_out[...] = jnp.sum(gated * gated, axis=1, keepdims=True)
    weighted = (stepped * head_lanes(jnp.exp(final - running), pairs)).astype(jnp.bfloat16)
    state[...] = state[...] * head_lanes(jnp.exp(final), pairs) + dot(
        write.T.astype(jnp.bfloat16), weighted
    )
    leaving_out[0, 0] = state[...].astype(jnp.bfloat16)


def gate_back_kernel(pairs, channels, last, edge_ref, before_ref, block_ref, raw_ref, taps, heads, gate_ref, y_ref, low_grad_ref, inverse_ref, coupling_ref, gain_ref, gate_grad_out, y_grad_out, gain_out, state_grad_out, window, state_grad, total):
    block = pl.program_id(1)
    first_of_all = (block == 0) & (pl.program_id(0) == 0)
    inner = pairs * 2 * MP

    @pl.when(block == 0)
    def _():
        state_grad[...] = jnp.zeros_like(state_grad)
        total[...] = jnp.zeros_like(total)

    @pl.when(first_of_all)
    def _():
        gain_out[...] = jnp.zeros_like(gain_out)

    gate = gate_ref[...]
    y = y_ref[...]
    low_grad = low_grad_ref[...]
    inverse = inverse_ref[...]
    sigmoid = jax.nn.sigmoid(gate)
    silu = gate * sigmoid
    gated = y * silu
    normed = gated * inverse
    gain_out[0:1, :] += jnp.sum(low_grad * normed, axis=0, keepdims=True)
    gated_grad = inverse * (
        gain_ref[0:1, :] * low_grad - normed * (inverse * coupling_ref[...] / channels)
    )
    y_grad = (gated_grad * silu).astype(jnp.bfloat16)
    y_grad_out[...] = y_grad
    gate_grad_out[...] = (gated_grad * y * (sigmoid * (1.0 + gate * (1.0 - sigmoid)))).astype(
        jnp.bfloat16
    )
    lanes = slice(inner + NS, inner + 2 * NS)
    load_window(window, edge_ref, before_ref, block_ref, block == 0)
    read = window_conv(window, taps, lanes)
    read = read * jax.nn.sigmoid(read)
    _, running, _, _ = step_values(raw_ref[...], heads[...])
    scaled = (
        y_grad.astype(jnp.float32) * head_lanes(jnp.exp(total[...] + running), pairs)
    ).astype(jnp.bfloat16)
    state_grad[...] += dot(read.T.astype(jnp.bfloat16), scaled)
    total[...] = total[...] + running[SPAN - 1 : SPAN, :]

    @pl.when(block == last)
    def _():
        state_grad_out[0] = state_grad[...].astype(jnp.bfloat16)


def backward_kernel(pairs, last, edge_ref, before_ref, block_ref, raw_ref, taps, heads, skip_ref, later_ref, entering_ref, leaving_ref, y_ref, y_grad_ref, conv_grad_out, step_grad_out, front_out, taps_out, heads_out, skip_out, window, state_grad, slopes):
    block = last - pl.program_id(1)
    first_step = pl.program_id(1) == 0
    inner = pairs * 2 * MP

    @pl.when(first_step)
    def _():
        state_grad[...] = later_ref[0].astype(jnp.float32)
        slopes[SPAN:, :] = jnp.zeros((8, slopes.shape[1]), jnp.float32)

    @pl.when(first_step & (pl.program_id(0) == 0))
    def _():
        taps_out[...] = jnp.zeros_like(taps_out)
        heads_out[...] = jnp.zeros_like(heads_out)
        skip_out[...] = jnp.zeros_like(skip_out)

    load_window(window, edge_ref, before_ref, block_ref, block == 0)
    before_silu = window_conv(window, taps, slice(0, inner + 2 * NS))
    sigmoid = jax.nn.sigmoid(before_silu)
    conv = before_silu * sigmoid
    head_x = conv[:, :inner]
    write = conv[:, inner : inner + NS]
    read = conv[:, inner + NS :]
    write_low = write.astype(jnp.bfloat16)
    read_low = read.astype(jnp.bfloat16)
    size, running, rate, argument = step_values(raw_ref[...], heads[...])
    running_t = running.T
    final = running[SPAN - 1 : SPAN, :]
    mask = lower_ones()
    mask_t = lower_ones(True)
    product = dot_t(read_low, write_low)
    product_t = dot_t(write_low, read_low)
    grad_low = y_grad_ref[...]
    grad = grad_low.astype(jnp.float32)
    entering = entering_ref[0, 0]
    state_low = state_grad[...].astype(jnp.bfloat16)
    grown = head_lanes(jnp.exp(running), pairs)
    tail = head_lanes(jnp.exp(final - running), pairs)
    size_lanes = head_lanes(size, pairs)
    stepped = head_x * size_lanes
    stepped_low = stepped.astype(jnp.bfloat16)
    from_state = dot(write_low, state_low) * tail
    product_grad = jnp.zeros((SPAN, SPAN), jnp.float32)
    slope_parts = []
    lane = lax.broadcasted_iota(jnp.int32, (SPAN, 2 * MP), 1)
    for pair in range(pairs):
        lanes = slice(pair * 2 * MP, (pair + 1) * 2 * MP)
        pair_grad = grad_low[:, lanes]
        mixing_t = []
        for side in (0, 1):
            head = 2 * pair + side
            column = running[:, head : head + 1]
            row = running_t[head : head + 1, :]
            decay = jnp.exp(jnp.where(mask, column - row, MASKED))
            decay_t = jnp.exp(jnp.where(mask_t, row - column, MASKED))
            mixing_t.append((product_t * decay_t).astype(jnp.bfloat16))
            own = (lane < MP) if side == 0 else (lane >= MP)
            one_head = jnp.where(own, pair_grad, jnp.zeros_like(pair_grad))
            product_grad = product_grad + dot_t(one_head, stepped_low[:, lanes]) * decay
        slope_parts.append(dot(jnp.concatenate(mixing_t, axis=1), stacked_pair(pair_grad)))
    slope = jnp.concatenate(slope_parts, axis=1) + from_state
    skip = skip_ref[0:1, :]
    x_grad = size_lanes * slope + skip * grad
    skip_out[0:1, :] += jnp.sum(grad * head_x, axis=0, keepdims=True)
    owner = lax.broadcasted_iota(jnp.int32, (inner, SPAN), 0) // MP
    ones = (owner == lax.broadcasted_iota(jnp.int32, (inner, SPAN), 1)).astype(jnp.bfloat16)
    y_scan = y_ref[...] - skip * head_x
    running_grad = split_dot(grad * y_scan - stepped * slope, ones)
    size_direct = split_dot(head_x * slope, ones)
    at_end = jnp.sum(
        state_grad[...] * leaving_ref[0, 0].astype(jnp.float32), axis=0, keepdims=True
    )
    at_end = split_dot(jnp.broadcast_to(at_end, (8, inner)), ones)[0:1, :]
    rate_grad = exact_dot(mask_t.astype(jnp.float32), running_grad) + at_end
    size_grad = size_direct + rate_grad * heads[1:2, :]
    valid = lax.broadcasted_iota(jnp.int32, (SPAN, SPAN), 1) < 2 * pairs
    raw_grad = jnp.where(valid, size_grad * jax.nn.sigmoid(argument), 0.0)
    step_grad_out[...] = raw_grad.astype(jnp.bfloat16)
    heads_out[0:1, :] += jnp.sum(raw_grad, axis=0, keepdims=True)
    heads_out[1:2, :] += jnp.sum(rate_grad * rate, axis=0, keepdims=True)
    grown_grad = (grad * grown).astype(jnp.bfloat16)
    product_grad_low = product_grad.astype(jnp.bfloat16)
    read_grad = dot(product_grad_low, write_low) + dot_t(grown_grad, entering)
    write_grad = dot(product_grad.T.astype(jnp.bfloat16), read_low) + dot_t(
        (stepped * tail).astype(jnp.bfloat16), state_low
    )
    state_grad[...] = state_grad[...] * head_lanes(jnp.exp(final), pairs) + dot(
        read.T.astype(jnp.bfloat16), grown_grad
    )
    conv_slope = jnp.concatenate([x_grad, write_grad, read_grad], axis=1) * (
        sigmoid * (1.0 + before_silu * (1.0 - sigmoid))
    )
    slopes[0:SPAN, :] = conv_slope
    taps_out[TAPS : TAPS + 1, :] += jnp.sum(conv_slope, axis=0, keepdims=True)
    total = jnp.zeros_like(conv_slope)
    for k in range(TAPS):
        start = EDGE - TAPS + 1 + k
        taps_out[k : k + 1, :] += jnp.sum(
            conv_slope * window[start : start + SPAN, :], axis=0, keepdims=True
        )
        ahead = TAPS - 1 - k
        total = total + taps[k : k + 1, :] * slopes[ahead : ahead + SPAN, :]
    conv_grad_out[...] = total.astype(jnp.bfloat16)
    slopes[SPAN:, :] = conv_slope[0:8, :]

    @pl.when(block == 0)
    def _():
        front_out[0] = conv_slope[0:EDGE, :].astype(jnp.bfloat16)


class Mixer:
    def __init__(self, conv_in, edge, step_lin, taps, heads, skip, gate_z, seq_count, step_block):
        self.seqs = seq_count
        self.rows = conv_in.shape[0] // seq_count
        self.blocks = self.rows // SPAN
        self.inner = gate_z.shape[1]
        self.pairs = self.inner // (2 * MP)
        self.width = conv_in.shape[1]
        self.base = (edge, conv_in, conv_in, step_lin, taps, heads)
        self.step_block = step_block
        self.skip, self.gate_z = skip, gate_z
        self.grid = (seq_count, self.blocks)

    def where(self, reverse):
        blocks = self.blocks
        return (lambda g, b: blocks - 1 - b) if reverse else (lambda g, b: b)

    def base_specs(self, reverse=False):
        at, blocks, per = self.where(reverse), self.blocks, SPAN // EDGE
        width, column = self.width, self.step_block
        return [
            pl.BlockSpec((1, EDGE, width), lambda g, b: (g, 0, 0)),
            pl.BlockSpec(
                (EDGE, width), lambda g, b: (g * blocks * per + jnp.maximum(at(g, b) * per - 1, 0), 0)
            ),
            pl.BlockSpec((SPAN, width), lambda g, b: (g * blocks + at(g, b), 0)),
            pl.BlockSpec((SPAN, SPAN), lambda g, b: (g * blocks + at(g, b), column)),
            pl.BlockSpec((8, width), lambda g, b: (0, 0)),
            pl.BlockSpec((8, SPAN), lambda g, b: (0, 0)),
        ]

    def rows_spec(self, width, reverse=False, dtype=None):
        at, blocks = self.where(reverse), self.blocks
        return pl.BlockSpec((SPAN, width), lambda g, b: (g * blocks + at(g, b), 0))

    def const_spec(self, width, rows=8):
        return pl.BlockSpec((rows, width), lambda g, b: (0, 0))

    def seq_spec(self, rows, width):
        return pl.BlockSpec((1, rows, width), lambda g, b: (g, 0, 0))

    def cost(self, products, arrays):
        count = self.seqs * self.blocks
        return (
            2 * count * products * SPAN * SPAN * self.inner,
            arrays * self.seqs * self.rows * self.inner,
            count * 2 * self.pairs * SPAN * SPAN,
        )

    def shape(self, width, dtype):
        return jax.ShapeDtypeStruct((self.seqs * self.rows, width), dtype)

    def window(self):
        return pltpu.VMEM((SPAN + EDGE, self.width), jnp.float32)

    def states(self):
        inner, last = self.inner, self.blocks - 1
        return tall(
            functools.partial(state_kernel, self.pairs, last),
            self.grid,
            self.base_specs(),
            [self.seq_spec(NS, inner), self.seq_spec(1, SPAN)],
            [
                jax.ShapeDtypeStruct((self.seqs, NS, inner), jnp.bfloat16),
                jax.ShapeDtypeStruct((self.seqs, 1, SPAN), jnp.float32),
            ],
            [self.window(), pltpu.VMEM((NS, inner), jnp.float32), pltpu.VMEM((1, SPAN), jnp.float32)],
            *self.cost(1, 3),
        )(*self.base)

    def forward(self, incoming):
        inner, blocks = self.inner, self.blocks
        rows = self.rows_spec
        saved = pl.BlockSpec((1, 1, NS, inner), lambda g, b: (g, b, 0, 0))
        return tall(
            functools.partial(forward_kernel, self.pairs),
            self.grid,
            [*self.base_specs(), rows(inner), self.const_spec(inner), self.seq_spec(NS, inner)],
            [rows(inner), rows(inner), rows(1), saved, saved],
            [
                self.shape(inner, jnp.float32),
                self.shape(inner, jnp.float32),
                self.shape(1, jnp.float32),
                jax.ShapeDtypeStruct((self.seqs, blocks, NS, inner), jnp.bfloat16),
                jax.ShapeDtypeStruct((self.seqs, blocks, NS, inner), jnp.bfloat16),
            ],
            [self.window(), pltpu.VMEM((NS, inner), jnp.float32)],
            *self.cost(4, 18),
        )(*self.base, self.gate_z, self.skip, incoming)

    def gate_back(self, y, low_grad, inverse, coupling, gain, channels):
        inner, last = self.inner, self.blocks - 1
        rows = self.rows_spec
        return tall(
            functools.partial(gate_back_kernel, self.pairs, channels, last),
            self.grid,
            [
                *self.base_specs(),
                *(rows(width) for width in (inner, inner, inner, 1, 1)),
                self.const_spec(inner),
            ],
            [rows(inner), rows(inner), self.const_spec(inner), self.seq_spec(NS, inner)],
            [
                self.shape(inner, jnp.bfloat16),
                self.shape(inner, jnp.bfloat16),
                jax.ShapeDtypeStruct((8, inner), jnp.float32),
                jax.ShapeDtypeStruct((self.seqs, NS, inner), jnp.bfloat16),
            ],
            [self.window(), pltpu.VMEM((NS, inner), jnp.float32), pltpu.VMEM((1, SPAN), jnp.float32)],
            *self.cost(1, 20),
        )(*self.base, self.gate_z, y, low_grad, inverse, coupling, gain)

    def backward(self, later, entering, leaving, y, y_grad):
        inner, width, last = self.inner, self.width, self.blocks - 1
        saved = pl.BlockSpec((1, 1, NS, inner), lambda g, b: (g, last - b, 0, 0))
        back = functools.partial(self.rows_spec, reverse=True)
        return tall(
            functools.partial(backward_kernel, self.pairs, last),
            self.grid,
            [
                *self.base_specs(True),
                self.const_spec(inner),
                self.seq_spec(NS, inner),
                saved,
                saved,
                back(inner),
                back(inner),
            ],
            [
                back(width),
                back(SPAN),
                self.seq_spec(EDGE, width),
                self.const_spec(width),
                self.const_spec(SPAN),
                self.const_spec(inner),
            ],
            [
                self.shape(width, jnp.bfloat16),
                self.shape(SPAN, jnp.bfloat16),
                jax.ShapeDtypeStruct((self.seqs, EDGE, width), jnp.bfloat16),
                jax.ShapeDtypeStruct((8, width), jnp.float32),
                jax.ShapeDtypeStruct((8, SPAN), jnp.float32),
                jax.ShapeDtypeStruct((8, inner), jnp.float32),
            ],
            [
                self.window(),
                pltpu.VMEM((NS, inner), jnp.float32),
                pltpu.VMEM((SPAN + 8, width), jnp.float32),
            ],
            *self.cost(9, 16),
        )(*self.base, self.skip, later, entering, leaving, y, y_grad)


def shards(
    tokens,
    out_grad,
    norm_gains,
    query_weight,
    key_value_matrix,
    output_weight,
    mixer_weight,
    state_weight,
    step_weight,
    conv_inner,
    conv_state,
    step_bias,
    decay_log,
    skip_scale,
    gated_gain,
    mamba_weight,
    gateup_weight,
    down_weight,
):
    seq_count, row_count, model_width = tokens.shape
    total_rows = seq_count * row_count
    context_index = lax.axis_index("ctx")
    tensor_index = lax.axis_index("tp")
    tensor_count = lax.axis_size("tp")
    key_length = row_count * lax.axis_size("ctx")
    query_width = query_weight.shape[1]
    query_heads = query_width // HEAD_DIMENSION
    state_heads = step_bias.shape[0]
    inner_width = state_heads * MP
    hidden = down_weight.shape[0]
    own_rows = query_weight.shape[0]

    c_state = inner_width
    c_gate = c_state + 2 * NS
    c_query = c_gate + inner_width
    c_pair = c_query + query_width
    c_step = c_pair + 2 * HEAD_DIMENSION
    c_gain = c_step + state_heads
    pad = -(c_gain + 2) % 128
    mixer_parts = jnp.swapaxes(mixer_weight.reshape(own_rows, state_heads, 2, MP), 1, 2).reshape(
        own_rows, 2, inner_width
    )
    pack_conv = jnp.concatenate([mixer_parts[:, 1], state_weight], axis=1)
    pack_small = jnp.concatenate(
        [
            query_weight,
            key_value_matrix.reshape(own_rows, -1),
            step_weight,
            norm_gains.T,
            jnp.zeros((own_rows, pad), jnp.bfloat16),
        ],
        axis=1,
    )
    second_pack = jnp.concatenate(
        [gateup_weight.reshape(own_rows, 2 * hidden), down_weight.T, mamba_weight.T, output_weight.T],
        axis=1,
    )
    small_all, _ = gather_weights(pack_small, "xyz")
    conv_all, under_way = gather_weights(pack_conv, "zxy")
    gate_all, _ = gather_weights(mixer_parts[:, 0], "yzx")
    second_pack, _ = tie(second_pack, under_way)
    second_all = lax.all_gather(second_pack, WEIGHT_AXES, axis=0, tiled=True)
    gateup_all = second_all[:, : 2 * hidden]
    down_all = second_all[:, 2 * hidden : 3 * hidden]
    mix_all = second_all[:, 3 * hidden :]

    residual = tokens.astype(jnp.float32).reshape(total_rows, model_width)
    first_inverse = rms_inverse(residual)
    first_gain = small_all[:, c_gain - c_query].astype(jnp.float32)
    second_gain = small_all[:, c_gain + 1 - c_query].astype(jnp.float32)
    normed_one = (residual * first_inverse * first_gain).astype(jnp.bfloat16)
    cosines, sines = rope_tables(context_index * row_count, row_count, HEAD_DIMENSION)
    whole_cos = jnp.concatenate([cosines, cosines], axis=1)
    whole_sin = jnp.concatenate([-sines, sines], axis=1)
    tables = jnp.stack(
        [
            jnp.concatenate([whole_cos, whole_cos], axis=1),
            jnp.concatenate([whole_sin, whole_sin], axis=1),
            jnp.concatenate([whole_cos, jnp.ones_like(whole_cos)], axis=1),
            jnp.concatenate([whole_sin, jnp.zeros_like(whole_sin)], axis=1),
        ]
    )
    attention = Attention(
        tables,
        (context_index * row_count).astype(jnp.int32)[None],
        seq_count,
        row_count,
        key_length,
        query_heads,
    )
    conv_in = dot(normed_one, conv_all).astype(jnp.bfloat16)
    gate_z = dot(normed_one, gate_all)
    small_lin = dot(normed_one, small_all)
    rotated_query, local_pairs = attention.prepare(small_lin)
    all_pairs = gather_ctx(local_pairs.reshape(seq_count, row_count, -1), 1)
    conv_rows = conv_in.reshape(seq_count, row_count, c_gate)
    edge = shift_along(conv_rows[:, row_count - EDGE :], "ctx", 1)
    taps = jnp.pad(
        jnp.concatenate([conv_inner, conv_state], axis=1).astype(jnp.float32),
        ((0, 8 - conv_inner.shape[0]), (0, 0)),
    )
    head_rows = jnp.stack([step_bias.astype(jnp.float32), -jnp.exp(decay_log.astype(jnp.float32))])
    head_rows = jnp.pad(head_rows, ((0, 6), (0, SPAN - state_heads)))
    skip_rows = jnp.pad(jnp.repeat(skip_scale.astype(jnp.float32), MP)[None], ((0, 7), (0, 0)))
    mixer = Mixer(
        conv_in,
        edge,
        small_lin,
        taps,
        head_rows,
        skip_rows,
        gate_z,
        seq_count,
        (c_step - c_query) // SPAN,
    )
    final_state, total_rate = mixer.states()
    incoming = carry_over(total_rate, final_state, True)

    attended, log_totals = attention.forward(rotated_query, all_pairs)
    y_scan, gated, squares, entering, leaving = mixer.forward(incoming)
    gate_gain = gated_gain.astype(jnp.float32)
    square_sum = sum_over(squares, "tp")
    gate_inverse = lax.rsqrt(square_sum / (inner_width * tensor_count) + EPSILON)
    gated_low = (gated * gate_inverse * gate_gain).astype(jnp.bfloat16)
    mixed = jnp.concatenate([gated_low, attended], axis=1)
    branch = sum_over(dot_t(mixed, mix_all), "tp")
    middle = residual + branch
    second_inverse = rms_inverse(middle)
    normed_two = (middle * second_inverse * second_gain).astype(jnp.bfloat16)
    gate_val = dot(normed_two, gateup_all[:, :hidden])
    up_val = dot(normed_two, gateup_all[:, hidden:])
    sigmoid_gate = jax.nn.sigmoid(gate_val)
    silu_gate = gate_val * sigmoid_gate
    act_low = (silu_gate * up_val).astype(jnp.bfloat16)
    share_width = model_width // tensor_count
    feed_part = dot_t(act_low, down_all).astype(jnp.bfloat16)
    if tensor_count == 2:
        start_own = tensor_index * share_width
        own_part = lax.dynamic_slice_in_dim(feed_part, start_own, share_width, 1)
        other_part = lax.dynamic_slice_in_dim(feed_part, share_width - start_own, share_width, 1)
        feed_share = own_part.astype(jnp.float32) + lax.ppermute(
            other_part, "tp", [(0, 1), (1, 0)]
        ).astype(jnp.float32)
    else:
        feed_share = lax.psum_scatter(feed_part, "tp", scatter_dimension=1, tiled=True).astype(
            jnp.float32
        )
    middle_share = lax.dynamic_slice_in_dim(middle, tensor_index * share_width, share_width, 1)
    out_block = (
        (middle_share + feed_share).astype(jnp.bfloat16).reshape(seq_count, row_count, share_width)
    )
    cotangent = out_grad.reshape(total_rows, model_width)
    act_grad = dot(cotangent, down_all)
    gate_grad = (act_grad * up_val * sigmoid_gate * (1.0 + gate_val * (1.0 - sigmoid_gate))).astype(
        jnp.bfloat16
    )
    up_grad = (act_grad * silu_gate).astype(jnp.bfloat16)
    both_grads = jnp.concatenate([gate_grad, up_grad], axis=1)
    feed_grads = jnp.concatenate(
        [
            t_dot(normed_two, both_grads).astype(jnp.bfloat16),
            t_dot(cotangent, act_low).astype(jnp.bfloat16),
        ],
        axis=1,
    )
    feed_grads, both_grads = tie(feed_grads, both_grads)
    feed_total = lax.psum_scatter(feed_grads, WEIGHT_AXES, scatter_dimension=0, tiled=True)
    normed_two_grad = sum_over(dot_t(both_grads, gateup_all), "tp")
    second_back, second_gain_grad = norm_back(middle, second_inverse, second_gain, normed_two_grad)
    middle_grad = cotangent.astype(jnp.float32) + second_back
    branch_grad = middle_grad.astype(jnp.bfloat16)
    mixed_grads = t_dot(branch_grad, mixed).astype(jnp.bfloat16)
    branch_grad, mixed_grads = tie(branch_grad, mixed_grads)
    mix_sum = scatter_stage(scatter_begin(mixed_grads), "x")

    attended_grad = dot(branch_grad, mix_all[:, inner_width:]).astype(jnp.bfloat16)
    gated_low_grad = dot(branch_grad, mix_all[:, :inner_width])
    coupling = sum_over(
        jnp.sum(gated_low_grad * gate_gain * gated, axis=-1, keepdims=True), "tp"
    )
    gain_rows = jnp.pad(gate_gain[None], ((0, 7), (0, 0)))
    gate_z_grad, y_grad, gain_sums, incoming_grad = mixer.gate_back(
        y_scan, gated_low_grad, gate_inverse, coupling, gain_rows, inner_width * tensor_count
    )
    gated_gain_grad = gain_sums[0]
    later_grad = carry_over(total_rate, incoming_grad, False)
    query_lin_grad, pair_grad_all = attention.backward(
        rotated_query, all_pairs, log_totals, attended_grad
    )
    mix_value, pair_grad_all = tie(mix_sum[0], pair_grad_all)
    mix_sum = scatter_stage((mix_value, mix_sum[1]), "y")
    pair_grad = scatter_sum_ctx(pair_grad_all, 1)
    pair_lin_grad = attention.pair_back(pair_grad.reshape(total_rows, -1))
    early_grads = jnp.concatenate([gate_z_grad, query_lin_grad, pair_lin_grad], axis=1)
    early = t_dot(normed_one, early_grads).astype(jnp.bfloat16)
    small_all_early = small_all[:, : c_step - c_query]
    early_part = dot_t(gate_z_grad, gate_all) + dot_t(
        jnp.concatenate([query_lin_grad, pair_lin_grad], axis=1), small_all_early
    )
    mix_value, early, early_part, y_grad = tie(mix_sum[0], early, early_part, y_grad)
    mix_sum = scatter_stage((mix_value, mix_sum[1]), "z")
    early = scatter_stage(scatter_begin(early), "y")
    conv_grad, step_grad, front_slopes, tap_sums, head_sums, skip_sums = mixer.backward(
        later_grad, entering, leaving, y_scan, y_grad
    )
    early_value, mix_total, conv_grad = tie(early[0], scatter_end(mix_sum), conv_grad)
    early = scatter_stage((early_value, early[1]), "x")
    table_grad = tap_sums[: conv_inner.shape[0]]
    bias_grad = head_sums[0, :state_heads]
    decay_log_grad = head_sums[1, :state_heads]
    skip_grad = jnp.sum(skip_sums[0].reshape(state_heads, MP), axis=1)
    rim = TAPS - 1
    ahead = shift_along(front_slopes[:, :8], "ctx", -1).astype(jnp.float32)
    rim_grad = jnp.stack(
        [sum(taps[k] * ahead[:, i - k] for k in range(i + 1)) for i in range(rim)], axis=1
    )
    conv_grad = conv_grad.reshape(seq_count, row_count, c_gate)
    ending = conv_grad[:, row_count - rim :].astype(jnp.float32) + rim_grad
    conv_grad = lax.dynamic_update_slice_in_dim(
        conv_grad, ending.astype(jnp.bfloat16), row_count - rim, 1
    ).reshape(total_rows, c_gate)
    late_grads = jnp.concatenate([conv_grad, step_grad], axis=1)
    late = t_dot(normed_one, late_grads).astype(jnp.bfloat16)
    late_width = late.shape[1] // 2 // SPAN * SPAN
    late_one, late_two, late_grads = tie(late[:, :late_width], late[:, late_width:], late_grads)
    late_one = scatter_stage(scatter_begin(late_one), "y")
    late_two = scatter_stage(scatter_begin(late_two), "x")
    normed_one_part = (
        early_part + dot_t(conv_grad, conv_all) + dot_t(step_grad, small_all[:, c_step - c_query :])
    )
    late_value, early_value, normed_one_part = tie(late_one[0], early[0], normed_one_part)
    late_one = scatter_stage((late_value, late_one[1]), "x")
    late_two = scatter_stage(late_two, "y")
    early = scatter_stage((early_value, early[1]), "z")
    normed_one_grad = sum_over(normed_one_part, "tp")
    late_total = jnp.concatenate(
        [scatter_end(scatter_stage(late_one, "z")), scatter_end(scatter_stage(late_two, "z"))], axis=1
    )
    early_total = scatter_end(early)
    first_back, first_gain_grad = norm_back(residual, first_inverse, first_gain, normed_one_grad)
    tokens_grad = (middle_grad + first_back).reshape(seq_count, row_count, model_width)

    state_table = sum_over(table_grad[:, inner_width:], "tp")
    flat = jnp.concatenate(
        [
            table_grad[:, :inner_width].reshape(-1),
            state_table.reshape(-1),
            gated_gain_grad,
            bias_grad,
            decay_log_grad,
            skip_grad,
        ]
    )
    flat_size = flat.shape[0]
    flat = jnp.pad(flat, (0, -flat_size % 1024)).reshape(-1, 128)
    for axis in WEIGHT_AXES:
        flat = sum_over(flat, axis)
    flat = flat.reshape(-1)
    tap_rows = conv_inner.shape[0]
    sizes = (
        tap_rows * inner_width,
        tap_rows * 2 * NS,
        inner_width,
        state_heads,
        state_heads,
        state_heads,
    )
    pieces, start = [], 0
    for size in sizes:
        pieces.append(flat[start : start + size])
        start += size
    conv_inner_total = pieces[0].reshape(tap_rows, inner_width)
    conv_state_total = pieces[1].reshape(tap_rows, 2 * NS)
    gated_total, bias_total, decay_total, skip_total = pieces[2:6]
    gain_total = jnp.stack([scatter_gain(first_gain_grad), scatter_gain(second_gain_grad)])

    wide_two = feed_total.astype(jnp.float32)
    mixer_total = jnp.stack(
        [
            early_total[:, :inner_width].reshape(own_rows, state_heads, MP),
            late_total[:, :inner_width].reshape(own_rows, state_heads, MP),
        ],
        axis=2,
    ).reshape(own_rows, state_heads, 2 * MP)
    state_weight_total = sum_over(late_total[:, c_state:c_gate], "tp")
    return (
        out_block,
        tokens_grad,
        gain_total,
        early_total[:, inner_width : inner_width + query_width],
        early_total[:, inner_width + query_width :].reshape(own_rows, 1, 2 * HEAD_DIMENSION),
        mix_total[:, inner_width:].T,
        mixer_total,
        state_weight_total,
        late_total[:, c_gate : c_gate + state_heads],
        conv_inner_total,
        conv_state_total,
        bias_total,
        decay_total,
        skip_total,
        gated_total,
        mix_total[:, :inner_width].T,
        wide_two[:, : 2 * hidden].reshape(own_rows, 2, hidden),
        wide_two[:, 2 * hidden : 3 * hidden].T,
    )


def solution(mesh):
    in_specs = (
        P("fsdp", "ctx", None),
        P("fsdp", "ctx", None),
        P(None, ("fsdp", "ctx")),
        P(("fsdp", "ctx"), "tp"),
        P(("fsdp", "ctx"), "tp", None),
        P("tp", ("fsdp", "ctx")),
        P(("fsdp", "ctx"), "tp", None),
        P(("fsdp", "ctx"), None),
        P(("fsdp", "ctx"), "tp"),
        P(None, "tp"),
        P(),
        P("tp"),
        P("tp"),
        P("tp"),
        P("tp"),
        P("tp", ("fsdp", "ctx")),
        P(("fsdp", "ctx"), None, "tp"),
        P("tp", ("fsdp", "ctx")),
    )
    out_specs = (
        P("fsdp", "ctx", "tp"),
        P("fsdp", "ctx", None),
        P(None, ("fsdp", "ctx")),
        P(("fsdp", "ctx"), "tp"),
        P(("fsdp", "ctx"), "tp", None),
        P("tp", ("fsdp", "ctx")),
        P(("fsdp", "ctx"), "tp", None),
        P(("fsdp", "ctx"), None),
        P(("fsdp", "ctx"), "tp"),
        P(None, "tp"),
        P(),
        P("tp"),
        P("tp"),
        P("tp"),
        P("tp"),
        P("tp", ("fsdp", "ctx")),
        P(("fsdp", "ctx"), None, "tp"),
        P("tp", ("fsdp", "ctx")),
    )
    return jax.shard_map(shards, mesh=mesh, in_specs=in_specs, out_specs=out_specs, check_vma=False)
```

```python
import functools

import jax
import jax.numpy as jnp
from jax import lax
from jax.experimental import pallas as pl
from jax.experimental.pallas import tpu as pltpu
from jax.sharding import PartitionSpec as P

HEAD_DIMENSION = 64
MP = 64
NS = 128
SPAN = 128


EPSILON = 1e-05
HIGHEST = lax.Precision.HIGHEST
MASKED = -1e30
ROPE_BASE = 10000.0
WEIGHT_AXES = ("fsdp", "ctx")
VMEM_LIMIT = 48 * 1024 * 1024
TAPS = 4
EDGE = 16


def shift_along(block, axis, distance):
    devices = range(lax.axis_size(axis))
    route = [(i - distance, i) for i in devices if i - distance in devices]
    return lax.ppermute(block, axis, route)


def sum_over(value, axis):
    count = lax.axis_size(axis)
    if count & (count - 1):
        return lax.psum(value, axis)
    stride = 1
    while stride < count:
        other = lax.ppermute(value, axis, [(i, i ^ stride) for i in range(count)])
        value = value + other
        stride *= 2
    return value


def gather_ctx(block, dim):
    count = lax.axis_size("ctx")
    if count == 1:
        return block
    if count > 2:
        return lax.all_gather(block, "ctx", axis=dim, tiled=True)
    other = lax.ppermute(block, "ctx", [(0, 1), (1, 0)])
    first = lax.axis_index("ctx") == 0
    return jnp.concatenate(
        [jnp.where(first, block, other), jnp.where(first, other, block)], axis=dim
    )


def scatter_sum_ctx(whole, dim):
    count = lax.axis_size("ctx")
    if count == 1:
        return whole
    if count > 2:
        return lax.psum_scatter(whole, "ctx", scatter_dimension=dim, tiled=True)
    half = whole.shape[dim] // 2
    low = lax.slice_in_dim(whole, 0, half, axis=dim)
    high = lax.slice_in_dim(whole, half, 2 * half, axis=dim)
    first = lax.axis_index("ctx") == 0
    kept = jnp.where(first, low, high)
    sent = jnp.where(first, high, low)
    return kept + lax.ppermute(sent, "ctx", [(0, 1), (1, 0)])


def carry_over(total_rate, state, forward):
    count = lax.axis_size("ctx")
    if count <= 2:
        return shift_along(state, "ctx", 1 if forward else -1)
    place = lax.axis_index("ctx")
    heads = state.shape[2] // MP
    decay = jnp.exp(total_rate[:, :, :heads]).astype(jnp.bfloat16)
    decays = jnp.repeat(lax.all_gather(decay, "ctx").astype(jnp.float32), MP, axis=3)
    states = lax.all_gather(state, "ctx").astype(jnp.float32)
    total = jnp.zeros(state.shape, jnp.float32)
    order = range(count) if forward else range(count - 1, -1, -1)
    for k in order:
        reached = k < place if forward else k > place
        total = jnp.where(reached, decays[k] * total + states[k], total)
    return total.astype(jnp.bfloat16)


def torus_route(step):
    def index(z, x, y):
        return (z * 2 + x) * 2 + y

    return [
        (index(z, x, y), index(*step(z, x, y)))
        for z in range(4)
        for x in range(2)
        for y in range(2)
    ]


def across(value, name, hop=1):
    step = {
        "x": lambda z, x, y: (z, 1 - x, y),
        "y": lambda z, x, y: (z, x, 1 - y),
        "z": lambda z, x, y: ((z + hop) % 4, x, y),
    }[name]
    return lax.ppermute(value, WEIGHT_AXES, torus_route(step))


def is_torus():
    return lax.axis_size("fsdp") == 8 and lax.axis_size("ctx") == 2


def torus_place():
    fsdp = lax.axis_index("fsdp")
    return {"z": fsdp // 2, "x": fsdp % 2, "y": lax.axis_index("ctx")}


def gather_weights(shard, order):
    if not is_torus():
        return lax.all_gather(shard, WEIGHT_AXES, axis=0, tiled=True), shard
    place = torus_place()
    done = ""
    value = shard
    early = None
    for name in order:
        spot = sum(1 for other in "zxy" if other in done and "zxy".index(other) < "zxy".index(name))
        if name == "z":
            parts = [value] + [across(value, "z", hop) for hop in (1, 2, 3)]
            gathered = jnp.zeros((4, *value.shape), value.dtype)
            for hop, part in enumerate(parts):
                gathered = lax.dynamic_update_index_in_dim(
                    gathered, part, (place["z"] - hop) % 4, 0
                )
            value = gathered
        else:
            other = across(value, name)
            low = place[name] == 0
            value = jnp.stack(
                [jnp.where(low, value, other), jnp.where(low, other, value)], axis=spot
            )
        done += name
        early = value if early is None else early
    return value.reshape(-1, shard.shape[1]), early


def scatter_begin(whole):
    if not is_torus():
        return lax.psum_scatter(whole, WEIGHT_AXES, scatter_dimension=0, tiled=True), ""
    return whole.reshape(4, 2, 2, -1, whole.shape[1]), "zxy"


def scatter_stage(state, name):
    value, left = state
    if not left:
        return state
    place = torus_place()[name]
    dim = left.index(name)

    def part(at):
        return lax.dynamic_index_in_dim(value, at, dim, keepdims=False)

    total = part(place).astype(jnp.float32)
    if name == "z":
        for hop in (1, 2, 3):
            total = total + across(part((place + hop) % 4), "z", hop).astype(jnp.float32)
    else:
        total = total + across(part(1 - place), name).astype(jnp.float32)
    left = left.replace(name, "")
    return (total.astype(jnp.bfloat16) if left else total), left


def scatter_end(state):
    return state[0].astype(jnp.float32)


def scatter_weights(whole, order):
    state = scatter_begin(whole)
    for name in order:
        state = scatter_stage(state, name)
    return scatter_end(state)


def scatter_gain(values):
    if not is_torus():
        return lax.psum_scatter(values, WEIGHT_AXES, scatter_dimension=0, tiled=True)
    place = torus_place()
    value = values.reshape(4, 4, -1)

    def part(array, at):
        return lax.dynamic_index_in_dim(array, at, 0, keepdims=False)

    total = part(value, place["z"])
    for hop in (1, 2, 3):
        total = total + across(part(value, (place["z"] + hop) % 4), "z", hop)
    result = part(total, 2 * place["x"] + place["y"])
    for dx, dy in ((0, 1), (1, 0), (1, 1)):
        sent = part(total, 2 * (place["x"] ^ dx) + (place["y"] ^ dy))
        route = torus_route(lambda z, x, y: (z, x ^ dx, y ^ dy))
        result = result + lax.ppermute(sent, WEIGHT_AXES, route)
    return result


def tie(*values):
    return lax.optimization_barrier(values)


def rms_inverse(values):
    return lax.rsqrt(jnp.mean(values * values, axis=-1, keepdims=True) + EPSILON)


def norm_back(values, inverse, gain_values, gradient):
    weighted = gradient * gain_values
    inner_sum = jnp.sum(weighted * values, axis=-1, keepdims=True) / values.shape[-1]
    return (
        inverse * weighted - values * inverse**3 * inner_sum,
        jnp.sum(gradient * values * inverse, axis=0),
    )


def rope_tables(first_place, place_count, head_width):
    position = (first_place + jnp.arange(place_count)).astype(jnp.float32)
    frequency = ROPE_BASE ** (-(jnp.arange(head_width // 2).astype(jnp.float32) * 2.0 / head_width))
    angles = position[:, None] * frequency[None, :]
    return (jnp.cos(angles), jnp.sin(angles))


def dot(a, b):
    return jnp.dot(a, b, preferred_element_type=jnp.float32)


def dot_t(a, b):
    return lax.dot_general(a, b, (((1,), (1,)), ((), ())), preferred_element_type=jnp.float32)


def t_dot(a, b):
    return lax.dot_general(a, b, (((0,), (0,)), ((), ())), preferred_element_type=jnp.float32)


def tall(kernel, grid, in_specs, out_specs, out_shape, scratch, flops, moved, exps):
    return pl.pallas_call(
        kernel,
        grid=grid,
        in_specs=in_specs,
        out_specs=out_specs,
        out_shape=out_shape,
        scratch_shapes=scratch,
        compiler_params=pltpu.CompilerParams(
            dimension_semantics=("arbitrary",) * len(grid), vmem_limit_bytes=VMEM_LIMIT
        ),
        cost_estimate=pl.CostEstimate(flops=flops, bytes_accessed=moved, transcendentals=exps),
    )


def turn(values, cosines, sines):
    rows, width = values.shape
    half = HEAD_DIMENSION // 2
    lane = lax.broadcasted_iota(jnp.int32, (rows, width), 1)
    swapped = jnp.where(
        lane % HEAD_DIMENSION < half, pltpu.roll(values, width - half, 1), pltpu.roll(values, half, 1)
    )
    times = width // cosines.shape[1]
    if times > 1:
        cosines = jnp.concatenate([cosines] * times, axis=1)
        sines = jnp.concatenate([sines] * times, axis=1)
    return values * cosines + swapped * sines


def turn_kernel(query_width, lin_ref, tables, query_out, pair_out):
    lin = lin_ref[...]
    query_out[...] = turn(lin[:, :query_width], tables[0], tables[1]).astype(jnp.bfloat16)
    pair_out[...] = turn(lin[:, query_width:], tables[2], tables[3]).astype(jnp.bfloat16)


def turn_back_kernel(grad_ref, tables, grad_out):
    grad = grad_ref[...].astype(jnp.float32)
    grad_out[...] = turn(grad, tables[2], -tables[3]).astype(jnp.bfloat16)


def one_head(tile_ref, head, to_left):
    start = head // 2 * 2 * HEAD_DIMENSION
    tile = tile_ref[:, start : start + 2 * HEAD_DIMENSION]
    is_left = head % 2 == 0
    if is_left != to_left:
        tile = pltpu.roll(tile.astype(jnp.float32), HEAD_DIMENSION, 1).astype(jnp.bfloat16)
    lane = lax.broadcasted_iota(jnp.int32, tile.shape, 1)
    kept = lane < HEAD_DIMENSION if to_left else lane >= HEAD_DIMENSION
    return jnp.where(kept, tile, jnp.zeros_like(tile))


def logits_t(pair, query, start, scale):
    logits = dot_t(pair, query) * scale
    key = lax.broadcasted_iota(jnp.int32, logits.shape, 0)
    place = lax.broadcasted_iota(jnp.int32, logits.shape, 1) + start
    return jnp.where(key <= place, logits, MASKED)


def join_heads(parts_t, on_left):
    tiles = []
    for left, right in zip(parts_t[::2], parts_t[1::2]):
        half = HEAD_DIMENSION
        pick = (lambda v: v[:half]) if on_left else (lambda v: v[half:])
        tiles.append(jnp.concatenate([pick(left), pick(right)], axis=0).T)
    return jnp.concatenate(tiles, axis=1)


def attend_kernel(heads, scale, start_ref, query_ref, pair_ref, out_ref, total_ref, pair_t):
    @pl.when(pl.program_id(1) == 0)
    def _():
        pair_t[...] = pair_ref[0].astype(jnp.float32).T.astype(jnp.bfloat16)

    pair = pair_ref[0]
    rows = query_ref.shape[0]
    start = start_ref[0] + pl.program_id(1) * rows
    outs = []
    for head in range(heads):
        logits = logits_t(pair, one_head(query_ref, head, True), start, scale)
        largest = jnp.max(logits, axis=0, keepdims=True)
        weights = jnp.exp(logits - largest)
        total = jnp.sum(weights, axis=0, keepdims=True)
        total_ref[0, head : head + 1, :] = largest + jnp.log(total)
        probs = (weights * (1.0 / total)).astype(jnp.bfloat16)
        outs.append(dot(pair_t[...], probs))
    out_ref[...] = join_heads(outs, False).astype(jnp.bfloat16)


def attend_back_kernel(heads, scale, last, start_ref, query_ref, pair_ref, total_ref, grad_ref, tables, query_out, pair_out, pair_t, pair_sum):
    @pl.when(pl.program_id(1) == 0)
    def _():
        pair_t[...] = pair_ref[0].astype(jnp.float32).T.astype(jnp.bfloat16)
        pair_sum[...] = jnp.zeros_like(pair_sum)

    pair = pair_ref[0]
    rows = query_ref.shape[0]
    start = start_ref[0] + pl.program_id(1) * rows
    outs = []
    for head in range(heads):
        query = one_head(query_ref, head, True)
        grad = one_head(grad_ref, head, False)
        probs = jnp.exp(
            logits_t(pair, query, start, scale) - total_ref[0, head : head + 1, :]
        )
        prob_grad = dot_t(pair, grad)
        inner_sum = jnp.sum(probs * prob_grad, axis=0, keepdims=True)
        logit_grad = (probs * (prob_grad - inner_sum)).astype(jnp.bfloat16)
        outs.append(dot(pair_t[...], logit_grad))
        pair_sum[...] += dot(logit_grad, query) * scale + dot(probs.astype(jnp.bfloat16), grad)
    query_grad = join_heads(outs, True) * scale
    query_out[...] = turn(query_grad, tables[0], -tables[1]).astype(jnp.bfloat16)

    @pl.when(pl.program_id(1) == last)
    def _():
        pair_out[0] = pair_sum[...].astype(jnp.bfloat16)


class Attention:
    def __init__(self, tables, start, seq_count, rows, keys, heads):
        self.tables, self.start = tables, start
        self.seqs, self.rows, self.keys, self.heads = seq_count, rows, keys, heads
        self.width = heads * HEAD_DIMENSION
        self.tile = min(256, rows)
        self.tiles = rows // self.tile
        self.scale = HEAD_DIMENSION ** (-0.5)

    def specs(self):
        tile, tiles, pair_width = self.tile, self.tiles, 2 * HEAD_DIMENSION
        return {
            "start": pl.BlockSpec(memory_space=pltpu.SMEM),
            "query": pl.BlockSpec((tile, self.width), lambda g, b: (g * tiles + b, 0)),
            "local": pl.BlockSpec((tile, pair_width), lambda g, b: (g * tiles + b, 0)),
            "lin": pl.BlockSpec((tile, self.width + pair_width), lambda g, b: (g * tiles + b, 0)),
            "pair": pl.BlockSpec((1, self.keys, pair_width), lambda g, b: (g, 0, 0)),
            "total": pl.BlockSpec((1, 8, tile), lambda g, b: (g, 0, b)),
            "tables": pl.BlockSpec((4, tile, 2 * HEAD_DIMENSION), lambda g, b: (0, b, 0)),
        }

    def call(self, kernel, ins, outs, shapes, scratch, products, operands):
        specs = self.specs()
        size = self.seqs * self.rows * self.keys * self.heads
        return tall(
            kernel,
            (self.seqs, self.tiles),
            [specs[name] for name in ins],
            [specs[name] for name in outs],
            shapes,
            scratch,
            2 * products * size * 2 * HEAD_DIMENSION,
            self.seqs * (self.rows + self.keys) * 1024,
            size if products else 0,
        )(*operands)

    def pair_shape(self):
        return jax.ShapeDtypeStruct((self.seqs * self.rows, 2 * HEAD_DIMENSION), jnp.bfloat16)

    def query_shape(self):
        return jax.ShapeDtypeStruct((self.seqs * self.rows, self.width), jnp.bfloat16)

    def prepare(self, lin):
        return self.call(
            functools.partial(turn_kernel, self.width),
            ("lin", "tables"),
            ("query", "local"),
            [self.query_shape(), self.pair_shape()],
            [],
            0,
            (lin, self.tables),
        )

    def forward(self, query, pairs):
        return self.call(
            functools.partial(attend_kernel, self.heads, self.scale),
            ("start", "query", "pair"),
            ("query", "total"),
            [self.query_shape(), jax.ShapeDtypeStruct((self.seqs, 8, self.rows), jnp.float32)],
            [pltpu.VMEM((2 * HEAD_DIMENSION, self.keys), jnp.bfloat16)],
            2,
            (self.start, query, pairs),
        )

    def backward(self, query, pairs, totals, grad):
        return self.call(
            functools.partial(attend_back_kernel, self.heads, self.scale, self.tiles - 1),
            ("start", "query", "pair", "total", "query", "tables"),
            ("query", "pair"),
            [
                self.query_shape(),
                jax.ShapeDtypeStruct((self.seqs, self.keys, 2 * HEAD_DIMENSION), jnp.bfloat16),
            ],
            [
                pltpu.VMEM((2 * HEAD_DIMENSION, self.keys), jnp.bfloat16),
                pltpu.VMEM((self.keys, 2 * HEAD_DIMENSION), jnp.float32),
            ],
            5,
            (self.start, query, pairs, totals, grad, self.tables),
        )

    def pair_back(self, grad):
        return self.call(
            turn_back_kernel,
            ("local", "tables"),
            ("local",),
            [self.pair_shape()],
            [],
            0,
            (grad, self.tables),
        )[0]


def lower_ones(transposed=False):
    rows = lax.broadcasted_iota(jnp.int32, (SPAN, SPAN), 0)
    columns = lax.broadcasted_iota(jnp.int32, (SPAN, SPAN), 1)
    return rows <= columns if transposed else rows >= columns


def exact_dot(a, b):
    return jnp.dot(a, b, preferred_element_type=jnp.float32, precision=HIGHEST)


def split_dot(a, b):
    high = a.astype(jnp.bfloat16)
    rest = (a - high.astype(jnp.float32)).astype(jnp.bfloat16)
    return dot(high, b) + dot(rest, b)


def pair_lanes(columns, pair):
    rows = columns.shape[0]
    lane = lax.broadcasted_iota(jnp.int32, (rows, 2 * MP), 1)
    left = jnp.broadcast_to(columns[:, 2 * pair : 2 * pair + 1], (rows, 2 * MP))
    right = jnp.broadcast_to(columns[:, 2 * pair + 1 : 2 * pair + 2], (rows, 2 * MP))
    return jnp.where(lane < MP, left, right)


def head_lanes(columns, pairs):
    return jnp.concatenate([pair_lanes(columns, j) for j in range(pairs)], axis=1)


def stacked_pair(values):
    lane = lax.broadcasted_iota(jnp.int32, values.shape, 1)
    zero = jnp.zeros_like(values)
    return jnp.concatenate(
        [jnp.where(lane < MP, values, zero), jnp.where(lane < MP, zero, values)], axis=0
    )


def load_window(window, edge_ref, before_ref, block_ref, first):
    edge = jnp.where(first, edge_ref[0].astype(jnp.float32), before_ref[...].astype(jnp.float32))
    window[0:EDGE, :] = edge
    window[EDGE:, :] = block_ref[...].astype(jnp.float32)


def window_conv(window, taps, lanes):
    total = taps[TAPS : TAPS + 1, lanes]
    for k in range(TAPS):
        start = EDGE - TAPS + 1 + k
        total = total + taps[k : k + 1, lanes] * window[start : start + SPAN, lanes]
    return total


def step_values(raw, heads):
    argument = raw + heads[0:1, :]
    size = jnp.maximum(argument, 0.0) + jnp.log1p(jnp.exp(-jnp.abs(argument)))
    rate = size * heads[1:2, :]
    return size, exact_dot(lower_ones().astype(jnp.float32), rate), rate, argument


def state_kernel(pairs, last, edge_ref, before_ref, block_ref, raw_ref, taps, heads, state_out, total_out, window, state, total):
    block = pl.program_id(1)
    inner = pairs * 2 * MP

    @pl.when(block == 0)
    def _():
        state[...] = jnp.zeros_like(state)
        total[...] = jnp.zeros_like(total)

    load_window(window, edge_ref, before_ref, block_ref, block == 0)
    conv = window_conv(window, taps, slice(0, inner + NS))
    conv = conv * jax.nn.sigmoid(conv)
    size, running, _, _ = step_values(raw_ref[...], heads[...])
    final = running[SPAN - 1 : SPAN, :]
    weight = jnp.exp(final - running) * size
    weighted = (conv[:, :inner] * head_lanes(weight, pairs)).astype(jnp.bfloat16)
    write_t = conv[:, inner:].T.astype(jnp.bfloat16)
    state[...] = state[...] * head_lanes(jnp.exp(final), pairs) + dot(write_t, weighted)
    total[...] = total[...] + final

    @pl.when(block == last)
    def _():
        state_out[0] = state[...].astype(jnp.bfloat16)
        total_out[0] = total[...]


def forward_kernel(pairs, edge_ref, before_ref, block_ref, raw_ref, taps, heads, gate_ref, skip_ref, incoming_ref, y_out, gated_out, square_out, entering_out, leaving_out, window, state):
    block = pl.program_id(1)
    inner = pairs * 2 * MP

    @pl.when(block == 0)
    def _():
        state[...] = incoming_ref[0].astype(jnp.float32)

    load_window(window, edge_ref, before_ref, block_ref, block == 0)
    conv = window_conv(window, taps, slice(0, inner + 2 * NS))
    conv = conv * jax.nn.sigmoid(conv)
    head_x = conv[:, :inner]
    write = conv[:, inner : inner + NS]
    read_low = conv[:, inner + NS :].astype(jnp.bfloat16)
    write_low = write.astype(jnp.bfloat16)
    size, running, _, _ = step_values(raw_ref[...], heads[...])
    running_t = running.T
    final = running[SPAN - 1 : SPAN, :]
    mask = lower_ones()
    product = dot_t(read_low, write_low)
    entering = state[...].astype(jnp.bfloat16)
    entering_out[0, 0] = entering
    carried = dot(read_low, entering) * head_lanes(jnp.exp(running), pairs)
    stepped = head_x * head_lanes(size, pairs)
    stepped_low = stepped.astype(jnp.bfloat16)
    inside = []
    for pair in range(pairs):
        mixing = []
        for head in (2 * pair, 2 * pair + 1):
            gap = running[:, head : head + 1] - running_t[head : head + 1, :]
            mixing.append((product * jnp.exp(jnp.where(mask, gap, MASKED))).astype(jnp.bfloat16))
        lanes = slice(pair * 2 * MP, (pair + 1) * 2 * MP)
        inside.append(dot(jnp.concatenate(mixing, axis=1), stacked_pair(stepped_low[:, lanes])))
    y = jnp.concatenate(inside, axis=1) + carried + skip_ref[0:1, :] * head_x
    gate = gate_ref[...]
    gated = y * (gate * jax.nn.sigmoid(gate))
    y_out[...] = y
    gated_out[...] = gated
    square_out[...] = jnp.sum(gated * gated, axis=1, keepdims=True)
    weighted = (stepped * head_lanes(jnp.exp(final - running), pairs)).astype(jnp.bfloat16)
    state[...] = state[...] * head_lanes(jnp.exp(final), pairs) + dot(
        write.T.astype(jnp.bfloat16), weighted
    )
    leaving_out[0, 0] = state[...].astype(jnp.bfloat16)


def gate_back_kernel(pairs, channels, last, edge_ref, before_ref, block_ref, raw_ref, taps, heads, gate_ref, y_ref, low_grad_ref, inverse_ref, coupling_ref, gain_ref, gate_grad_out, y_grad_out, gain_out, state_grad_out, window, state_grad, total):
    block = pl.program_id(1)
    first_of_all = (block == 0) & (pl.program_id(0) == 0)
    inner = pairs * 2 * MP

    @pl.when(block == 0)
    def _():
        state_grad[...] = jnp.zeros_like(state_grad)
        total[...] = jnp.zeros_like(total)

    @pl.when(first_of_all)
    def _():
        gain_out[...] = jnp.zeros_like(gain_out)

    gate = gate_ref[...]
    y = y_ref[...]
    low_grad = low_grad_ref[...]
    inverse = inverse_ref[...]
    sigmoid = jax.nn.sigmoid(gate)
    silu = gate * sigmoid
    gated = y * silu
    normed = gated * inverse
    gain_out[0:1, :] += jnp.sum(low_grad * normed, axis=0, keepdims=True)
    gated_grad = inverse * (
        gain_ref[0:1, :] * low_grad - normed * (inverse * coupling_ref[...] / channels)
    )
    y_grad = (gated_grad * silu).astype(jnp.bfloat16)
    y_grad_out[...] = y_grad
    gate_grad_out[...] = (gated_grad * y * (sigmoid * (1.0 + gate * (1.0 - sigmoid)))).astype(
        jnp.bfloat16
    )
    lanes = slice(inner + NS, inner + 2 * NS)
    load_window(window, edge_ref, before_ref, block_ref, block == 0)
    read = window_conv(window, taps, lanes)
    read = read * jax.nn.sigmoid(read)
    _, running, _, _ = step_values(raw_ref[...], heads[...])
    scaled = (
        y_grad.astype(jnp.float32) * head_lanes(jnp.exp(total[...] + running), pairs)
    ).astype(jnp.bfloat16)
    state_grad[...] += dot(read.T.astype(jnp.bfloat16), scaled)
    total[...] = total[...] + running[SPAN - 1 : SPAN, :]

    @pl.when(block == last)
    def _():
        state_grad_out[0] = state_grad[...].astype(jnp.bfloat16)


def backward_kernel(pairs, last, edge_ref, before_ref, block_ref, raw_ref, taps, heads, skip_ref, later_ref, entering_ref, leaving_ref, y_ref, y_grad_ref, conv_grad_out, step_grad_out, front_out, taps_out, heads_out, skip_out, window, state_grad, slopes):
    block = last - pl.program_id(1)
    first_step = pl.program_id(1) == 0
    inner = pairs * 2 * MP

    @pl.when(first_step)
    def _():
        state_grad[...] = later_ref[0].astype(jnp.float32)
        slopes[SPAN:, :] = jnp.zeros((8, slopes.shape[1]), jnp.float32)

    @pl.when(first_step & (pl.program_id(0) == 0))
    def _():
        taps_out[...] = jnp.zeros_like(taps_out)
        heads_out[...] = jnp.zeros_like(heads_out)
        skip_out[...] = jnp.zeros_like(skip_out)

    load_window(window, edge_ref, before_ref, block_ref, block == 0)
    before_silu = window_conv(window, taps, slice(0, inner + 2 * NS))
    sigmoid = jax.nn.sigmoid(before_silu)
    conv = before_silu * sigmoid
    head_x = conv[:, :inner]
    write = conv[:, inner : inner + NS]
    read = conv[:, inner + NS :]
    write_low = write.astype(jnp.bfloat16)
    read_low = read.astype(jnp.bfloat16)
    size, running, rate, argument = step_values(raw_ref[...], heads[...])
    running_t = running.T
    final = running[SPAN - 1 : SPAN, :]
    mask = lower_ones()
    mask_t = lower_ones(True)
    product = dot_t(read_low, write_low)
    product_t = dot_t(write_low, read_low)
    grad_low = y_grad_ref[...]
    grad = grad_low.astype(jnp.float32)
    entering = entering_ref[0, 0]
    state_low = state_grad[...].astype(jnp.bfloat16)
    grown = head_lanes(jnp.exp(running), pairs)
    tail = head_lanes(jnp.exp(final - running), pairs)
    size_lanes = head_lanes(size, pairs)
    stepped = head_x * size_lanes
    stepped_low = stepped.astype(jnp.bfloat16)
    from_state = dot(write_low, state_low) * tail
    product_grad = jnp.zeros((SPAN, SPAN), jnp.float32)
    slope_parts = []
    lane = lax.broadcasted_iota(jnp.int32, (SPAN, 2 * MP), 1)
    for pair in range(pairs):
        lanes = slice(pair * 2 * MP, (pair + 1) * 2 * MP)
        pair_grad = grad_low[:, lanes]
        mixing_t = []
        for side in (0, 1):
            head = 2 * pair + side
            column = running[:, head : head + 1]
            row = running_t[head : head + 1, :]
            decay = jnp.exp(jnp.where(mask, column - row, MASKED))
            decay_t = jnp.exp(jnp.where(mask_t, row - column, MASKED))
            mixing_t.append((product_t * decay_t).astype(jnp.bfloat16))
            own = (lane < MP) if side == 0 else (lane >= MP)
            one_head = jnp.where(own, pair_grad, jnp.zeros_like(pair_grad))
            product_grad = product_grad + dot_t(one_head, stepped_low[:, lanes]) * decay
        slope_parts.append(dot(jnp.concatenate(mixing_t, axis=1), stacked_pair(pair_grad)))
    slope = jnp.concatenate(slope_parts, axis=1) + from_state
    skip = skip_ref[0:1, :]
    x_grad = size_lanes * slope + skip * grad
    skip_out[0:1, :] += jnp.sum(grad * head_x, axis=0, keepdims=True)
    owner = lax.broadcasted_iota(jnp.int32, (inner, SPAN), 0) // MP
    ones = (owner == lax.broadcasted_iota(jnp.int32, (inner, SPAN), 1)).astype(jnp.bfloat16)
    y_scan = y_ref[...] - skip * head_x
    running_grad = split_dot(grad * y_scan - stepped * slope, ones)
    size_direct = split_dot(head_x * slope, ones)
    at_end = jnp.sum(
        state_grad[...] * leaving_ref[0, 0].astype(jnp.float32), axis=0, keepdims=True
    )
    at_end = split_dot(jnp.broadcast_to(at_end, (8, inner)), ones)[0:1, :]
    rate_grad = exact_dot(mask_t.astype(jnp.float32), running_grad) + at_end
    size_grad = size_direct + rate_grad * heads[1:2, :]
    valid = lax.broadcasted_iota(jnp.int32, (SPAN, SPAN), 1) < 2 * pairs
    raw_grad = jnp.where(valid, size_grad * jax.nn.sigmoid(argument), 0.0)
    step_grad_out[...] = raw_grad.astype(jnp.bfloat16)
    heads_out[0:1, :] += jnp.sum(raw_grad, axis=0, keepdims=True)
    heads_out[1:2, :] += jnp.sum(rate_grad * rate, axis=0, keepdims=True)
    grown_grad = (grad * grown).astype(jnp.bfloat16)
    product_grad_low = product_grad.astype(jnp.bfloat16)
    read_grad = dot(product_grad_low, write_low) + dot_t(grown_grad, entering)
    write_grad = dot(product_grad.T.astype(jnp.bfloat16), read_low) + dot_t(
        (stepped * tail).astype(jnp.bfloat16), state_low
    )
    state_grad[...] = state_grad[...] * head_lanes(jnp.exp(final), pairs) + dot(
        read.T.astype(jnp.bfloat16), grown_grad
    )
    conv_slope = jnp.concatenate([x_grad, write_grad, read_grad], axis=1) * (
        sigmoid * (1.0 + before_silu * (1.0 - sigmoid))
    )
    slopes[0:SPAN, :] = conv_slope
    taps_out[TAPS : TAPS + 1, :] += jnp.sum(conv_slope, axis=0, keepdims=True)
    total = jnp.zeros_like(conv_slope)
    for k in range(TAPS):
        start = EDGE - TAPS + 1 + k
        taps_out[k : k + 1, :] += jnp.sum(
            conv_slope * window[start : start + SPAN, :], axis=0, keepdims=True
        )
        ahead = TAPS - 1 - k
        total = total + taps[k : k + 1, :] * slopes[ahead : ahead + SPAN, :]
    conv_grad_out[...] = total.astype(jnp.bfloat16)
    slopes[SPAN:, :] = conv_slope[0:8, :]

    @pl.when(block == 0)
    def _():
        front_out[0] = conv_slope[0:EDGE, :].astype(jnp.bfloat16)


class Mixer:
    def __init__(self, conv_in, edge, step_lin, taps, heads, skip, gate_z, seq_count, step_block):
        self.seqs = seq_count
        self.rows = conv_in.shape[0] // seq_count
        self.blocks = self.rows // SPAN
        self.inner = gate_z.shape[1]
        self.pairs = self.inner // (2 * MP)
        self.width = conv_in.shape[1]
        self.base = (edge, conv_in, conv_in, step_lin, taps, heads)
        self.step_block = step_block
        self.skip, self.gate_z = skip, gate_z
        self.grid = (seq_count, self.blocks)

    def where(self, reverse):
        blocks = self.blocks
        return (lambda g, b: blocks - 1 - b) if reverse else (lambda g, b: b)

    def base_specs(self, reverse=False):
        at, blocks, per = self.where(reverse), self.blocks, SPAN // EDGE
        width, column = self.width, self.step_block
        return [
            pl.BlockSpec((1, EDGE, width), lambda g, b: (g, 0, 0)),
            pl.BlockSpec(
                (EDGE, width), lambda g, b: (g * blocks * per + jnp.maximum(at(g, b) * per - 1, 0), 0)
            ),
            pl.BlockSpec((SPAN, width), lambda g, b: (g * blocks + at(g, b), 0)),
            pl.BlockSpec((SPAN, SPAN), lambda g, b: (g * blocks + at(g, b), column)),
            pl.BlockSpec((8, width), lambda g, b: (0, 0)),
            pl.BlockSpec((8, SPAN), lambda g, b: (0, 0)),
        ]

    def rows_spec(self, width, reverse=False, dtype=None):
        at, blocks = self.where(reverse), self.blocks
        return pl.BlockSpec((SPAN, width), lambda g, b: (g * blocks + at(g, b), 0))

    def const_spec(self, width, rows=8):
        return pl.BlockSpec((rows, width), lambda g, b: (0, 0))

    def seq_spec(self, rows, width):
        return pl.BlockSpec((1, rows, width), lambda g, b: (g, 0, 0))

    def cost(self, products, arrays):
        count = self.seqs * self.blocks
        return (
            2 * count * products * SPAN * SPAN * self.inner,
            arrays * self.seqs * self.rows * self.inner,
            count * 2 * self.pairs * SPAN * SPAN,
        )

    def shape(self, width, dtype):
        return jax.ShapeDtypeStruct((self.seqs * self.rows, width), dtype)

    def window(self):
        return pltpu.VMEM((SPAN + EDGE, self.width), jnp.float32)

    def states(self):
        inner, last = self.inner, self.blocks - 1
        return tall(
            functools.partial(state_kernel, self.pairs, last),
            self.grid,
            self.base_specs(),
            [self.seq_spec(NS, inner), self.seq_spec(1, SPAN)],
            [
                jax.ShapeDtypeStruct((self.seqs, NS, inner), jnp.bfloat16),
                jax.ShapeDtypeStruct((self.seqs, 1, SPAN), jnp.float32),
            ],
            [self.window(), pltpu.VMEM((NS, inner), jnp.float32), pltpu.VMEM((1, SPAN), jnp.float32)],
            *self.cost(1, 3),
        )(*self.base)

    def forward(self, incoming):
        inner, blocks = self.inner, self.blocks
        rows = self.rows_spec
        saved = pl.BlockSpec((1, 1, NS, inner), lambda g, b: (g, b, 0, 0))
        return tall(
            functools.partial(forward_kernel, self.pairs),
            self.grid,
            [*self.base_specs(), rows(inner), self.const_spec(inner), self.seq_spec(NS, inner)],
            [rows(inner), rows(inner), rows(1), saved, saved],
            [
                self.shape(inner, jnp.float32),
                self.shape(inner, jnp.float32),
                self.shape(1, jnp.float32),
                jax.ShapeDtypeStruct((self.seqs, blocks, NS, inner), jnp.bfloat16),
                jax.ShapeDtypeStruct((self.seqs, blocks, NS, inner), jnp.bfloat16),
            ],
            [self.window(), pltpu.VMEM((NS, inner), jnp.float32)],
            *self.cost(4, 18),
        )(*self.base, self.gate_z, self.skip, incoming)

    def gate_back(self, y, low_grad, inverse, coupling, gain, channels):
        inner, last = self.inner, self.blocks - 1
        rows = self.rows_spec
        return tall(
            functools.partial(gate_back_kernel, self.pairs, channels, last),
            self.grid,
            [
                *self.base_specs(),
                *(rows(width) for width in (inner, inner, inner, 1, 1)),
                self.const_spec(inner),
            ],
            [rows(inner), rows(inner), self.const_spec(inner), self.seq_spec(NS, inner)],
            [
                self.shape(inner, jnp.bfloat16),
                self.shape(inner, jnp.bfloat16),
                jax.ShapeDtypeStruct((8, inner), jnp.float32),
                jax.ShapeDtypeStruct((self.seqs, NS, inner), jnp.bfloat16),
            ],
            [self.window(), pltpu.VMEM((NS, inner), jnp.float32), pltpu.VMEM((1, SPAN), jnp.float32)],
            *self.cost(1, 20),
        )(*self.base, self.gate_z, y, low_grad, inverse, coupling, gain)

    def backward(self, later, entering, leaving, y, y_grad):
        inner, width, last = self.inner, self.width, self.blocks - 1
        saved = pl.BlockSpec((1, 1, NS, inner), lambda g, b: (g, last - b, 0, 0))
        back = functools.partial(self.rows_spec, reverse=True)
        return tall(
            functools.partial(backward_kernel, self.pairs, last),
            self.grid,
            [
                *self.base_specs(True),
                self.const_spec(inner),
                self.seq_spec(NS, inner),
                saved,
                saved,
                back(inner),
                back(inner),
            ],
            [
                back(width),
                back(SPAN),
                self.seq_spec(EDGE, width),
                self.const_spec(width),
                self.const_spec(SPAN),
                self.const_spec(inner),
            ],
            [
                self.shape(width, jnp.bfloat16),
                self.shape(SPAN, jnp.bfloat16),
                jax.ShapeDtypeStruct((self.seqs, EDGE, width), jnp.bfloat16),
                jax.ShapeDtypeStruct((8, width), jnp.float32),
                jax.ShapeDtypeStruct((8, SPAN), jnp.float32),
                jax.ShapeDtypeStruct((8, inner), jnp.float32),
            ],
            [
                self.window(),
                pltpu.VMEM((NS, inner), jnp.float32),
                pltpu.VMEM((SPAN + 8, width), jnp.float32),
            ],
            *self.cost(9, 16),
        )(*self.base, self.skip, later, entering, leaving, y, y_grad)


def shards(
    tokens,
    out_grad,
    norm_gains,
    query_weight,
    key_value_matrix,
    output_weight,
    mixer_weight,
    state_weight,
    step_weight,
    conv_inner,
    conv_state,
    step_bias,
    decay_log,
    skip_scale,
    gated_gain,
    mamba_weight,
    gateup_weight,
    down_weight,
):
    seq_count, row_count, model_width = tokens.shape
    total_rows = seq_count * row_count
    context_index = lax.axis_index("ctx")
    tensor_index = lax.axis_index("tp")
    tensor_count = lax.axis_size("tp")
    key_length = row_count * lax.axis_size("ctx")
    query_width = query_weight.shape[1]
    query_heads = query_width // HEAD_DIMENSION
    state_heads = step_bias.shape[0]
    inner_width = state_heads * MP
    hidden = down_weight.shape[0]
    own_rows = query_weight.shape[0]

    c_state = inner_width
    c_gate = c_state + 2 * NS
    c_query = c_gate + inner_width
    c_pair = c_query + query_width
    c_step = c_pair + 2 * HEAD_DIMENSION
    c_gain = c_step + state_heads
    pad = -(c_gain + 2) % 128
    mixer_parts = jnp.swapaxes(mixer_weight.reshape(own_rows, state_heads, 2, MP), 1, 2).reshape(
        own_rows, 2, inner_width
    )
    pack_conv = jnp.concatenate([mixer_parts[:, 1], state_weight], axis=1)
    pack_small = jnp.concatenate(
        [
            query_weight,
            key_value_matrix.reshape(own_rows, -1),
            step_weight,
            norm_gains.T,
            jnp.zeros((own_rows, pad), jnp.bfloat16),
        ],
        axis=1,
    )
    second_pack = jnp.concatenate(
        [gateup_weight.reshape(own_rows, 2 * hidden), down_weight.T, mamba_weight.T, output_weight.T],
        axis=1,
    )
    small_all, _ = gather_weights(pack_small, "xyz")
    conv_all, under_way = gather_weights(pack_conv, "zxy")
    gate_all, _ = gather_weights(mixer_parts[:, 0], "yzx")
    second_pack, _ = tie(second_pack, under_way)
    second_all = lax.all_gather(second_pack, WEIGHT_AXES, axis=0, tiled=True)
    gateup_all = second_all[:, : 2 * hidden]
    down_all = second_all[:, 2 * hidden : 3 * hidden]
    mix_all = second_all[:, 3 * hidden :]

    residual = tokens.astype(jnp.float32).reshape(total_rows, model_width)
    first_inverse = rms_inverse(residual)
    first_gain = small_all[:, c_gain - c_query].astype(jnp.float32)
    second_gain = small_all[:, c_gain + 1 - c_query].astype(jnp.float32)
    normed_one = (residual * first_inverse * first_gain).astype(jnp.bfloat16)
    cosines, sines = rope_tables(context_index * row_count, row_count, HEAD_DIMENSION)
    whole_cos = jnp.concatenate([cosines, cosines], axis=1)
    whole_sin = jnp.concatenate([-sines, sines], axis=1)
    tables = jnp.stack(
        [
            jnp.concatenate([whole_cos, whole_cos], axis=1),
            jnp.concatenate([whole_sin, whole_sin], axis=1),
            jnp.concatenate([whole_cos, jnp.ones_like(whole_cos)], axis=1),
            jnp.concatenate([whole_sin, jnp.zeros_like(whole_sin)], axis=1),
        ]
    )
    attention = Attention(
        tables,
        (context_index * row_count).astype(jnp.int32)[None],
        seq_count,
        row_count,
        key_length,
        query_heads,
    )
    conv_in = dot(normed_one, conv_all).astype(jnp.bfloat16)
    gate_z = dot(normed_one, gate_all)
    small_lin = dot(normed_one, small_all)
    rotated_query, local_pairs = attention.prepare(small_lin)
    all_pairs = gather_ctx(local_pairs.reshape(seq_count, row_count, -1), 1)
    conv_rows = conv_in.reshape(seq_count, row_count, c_gate)
    edge = shift_along(conv_rows[:, row_count - EDGE :], "ctx", 1)
    taps = jnp.pad(
        jnp.concatenate([conv_inner, conv_state], axis=1).astype(jnp.float32),
        ((0, 8 - conv_inner.shape[0]), (0, 0)),
    )
    head_rows = jnp.stack([step_bias.astype(jnp.float32), -jnp.exp(decay_log.astype(jnp.float32))])
    head_rows = jnp.pad(head_rows, ((0, 6), (0, SPAN - state_heads)))
    skip_rows = jnp.pad(jnp.repeat(skip_scale.astype(jnp.float32), MP)[None], ((0, 7), (0, 0)))
    mixer = Mixer(
        conv_in,
        edge,
        small_lin,
        taps,
        head_rows,
        skip_rows,
        gate_z,
        seq_count,
        (c_step - c_query) // SPAN,
    )
    final_state, total_rate = mixer.states()
    incoming = carry_over(total_rate, final_state, True)

    attended, log_totals = attention.forward(rotated_query, all_pairs)
    y_scan, gated, squares, entering, leaving = mixer.forward(incoming)
    gate_gain = gated_gain.astype(jnp.float32)
    square_sum = sum_over(squares, "tp")
    gate_inverse = lax.rsqrt(square_sum / (inner_width * tensor_count) + EPSILON)
    gated_low = (gated * gate_inverse * gate_gain).astype(jnp.bfloat16)
    mixed = jnp.concatenate([gated_low, attended], axis=1)
    branch = sum_over(dot_t(mixed, mix_all), "tp")
    middle = residual + branch
    second_inverse = rms_inverse(middle)
    normed_two = (middle * second_inverse * second_gain).astype(jnp.bfloat16)
    gate_val = dot(normed_two, gateup_all[:, :hidden])
    up_val = dot(normed_two, gateup_all[:, hidden:])
    sigmoid_gate = jax.nn.sigmoid(gate_val)
    silu_gate = gate_val * sigmoid_gate
    act_low = (silu_gate * up_val).astype(jnp.bfloat16)
    share_width = model_width // tensor_count
    feed_part = dot_t(act_low, down_all).astype(jnp.bfloat16)
    if tensor_count == 2:
        start_own = tensor_index * share_width
        own_part = lax.dynamic_slice_in_dim(feed_part, start_own, share_width, 1)
        other_part = lax.dynamic_slice_in_dim(feed_part, share_width - start_own, share_width, 1)
        feed_share = own_part.astype(jnp.float32) + lax.ppermute(
            other_part, "tp", [(0, 1), (1, 0)]
        ).astype(jnp.float32)
    else:
        feed_share = lax.psum_scatter(feed_part, "tp", scatter_dimension=1, tiled=True).astype(
            jnp.float32
        )
    middle_share = lax.dynamic_slice_in_dim(middle, tensor_index * share_width, share_width, 1)
    out_block = (
        (middle_share + feed_share).astype(jnp.bfloat16).reshape(seq_count, row_count, share_width)
    )
    cotangent = out_grad.reshape(total_rows, model_width)
    act_grad = dot(cotangent, down_all)
    gate_grad = (act_grad * up_val * sigmoid_gate * (1.0 + gate_val * (1.0 - sigmoid_gate))).astype(
        jnp.bfloat16
    )
    up_grad = (act_grad * silu_gate).astype(jnp.bfloat16)
    both_grads = jnp.concatenate([gate_grad, up_grad], axis=1)
    feed_grads = jnp.concatenate(
        [
            t_dot(normed_two, gate_grad).astype(jnp.bfloat16),
            t_dot(normed_two, up_grad).astype(jnp.bfloat16),
            t_dot(cotangent, act_low).astype(jnp.bfloat16),
        ],
        axis=1,
    )
    feed_grads, both_grads = tie(feed_grads, both_grads)
    feed_total = lax.psum_scatter(feed_grads, WEIGHT_AXES, scatter_dimension=0, tiled=True)
    normed_two_grad = sum_over(dot_t(both_grads, gateup_all), "tp")
    second_back, second_gain_grad = norm_back(middle, second_inverse, second_gain, normed_two_grad)
    middle_grad = cotangent.astype(jnp.float32) + second_back
    branch_grad = middle_grad.astype(jnp.bfloat16)
    mixed_grads = t_dot(branch_grad, mixed).astype(jnp.bfloat16)
    branch_grad, mixed_grads = tie(branch_grad, mixed_grads)
    mix_sum = scatter_stage(scatter_begin(mixed_grads), "x")

    attended_grad = dot(branch_grad, mix_all[:, inner_width:]).astype(jnp.bfloat16)
    gated_low_grad = dot(branch_grad, mix_all[:, :inner_width])
    coupling = sum_over(
        jnp.sum(gated_low_grad * gate_gain * gated, axis=-1, keepdims=True), "tp"
    )
    gain_rows = jnp.pad(gate_gain[None], ((0, 7), (0, 0)))
    gate_z_grad, y_grad, gain_sums, incoming_grad = mixer.gate_back(
        y_scan, gated_low_grad, gate_inverse, coupling, gain_rows, inner_width * tensor_count
    )
    gated_gain_grad = gain_sums[0]
    later_grad = carry_over(total_rate, incoming_grad, False)
    query_lin_grad, pair_grad_all = attention.backward(
        rotated_query, all_pairs, log_totals, attended_grad
    )
    mix_value, pair_grad_all = tie(mix_sum[0], pair_grad_all)
    mix_sum = scatter_stage((mix_value, mix_sum[1]), "y")
    pair_grad = scatter_sum_ctx(pair_grad_all, 1)
    pair_lin_grad = attention.pair_back(pair_grad.reshape(total_rows, -1))
    early_grads = jnp.concatenate([gate_z_grad, query_lin_grad, pair_lin_grad], axis=1)
    early = t_dot(normed_one, early_grads).astype(jnp.bfloat16)
    small_all_early = small_all[:, : c_step - c_query]
    early_part = dot_t(gate_z_grad, gate_all) + dot_t(
        jnp.concatenate([query_lin_grad, pair_lin_grad], axis=1), small_all_early
    )
    mix_value, early, early_part, y_grad = tie(mix_sum[0], early, early_part, y_grad)
    mix_sum = scatter_stage((mix_value, mix_sum[1]), "z")
    early = scatter_stage(scatter_begin(early), "y")
    conv_grad, step_grad, front_slopes, tap_sums, head_sums, skip_sums = mixer.backward(
        later_grad, entering, leaving, y_scan, y_grad
    )
    early_value, mix_total, conv_grad = tie(early[0], scatter_end(mix_sum), conv_grad)
    early = scatter_stage((early_value, early[1]), "x")
    table_grad = tap_sums[: conv_inner.shape[0]]
    bias_grad = head_sums[0, :state_heads]
    decay_log_grad = head_sums[1, :state_heads]
    skip_grad = jnp.sum(skip_sums[0].reshape(state_heads, MP), axis=1)
    rim = TAPS - 1
    ahead = shift_along(front_slopes[:, :8], "ctx", -1).astype(jnp.float32)
    rim_grad = jnp.stack(
        [sum(taps[k] * ahead[:, i - k] for k in range(i + 1)) for i in range(rim)], axis=1
    )
    conv_grad = conv_grad.reshape(seq_count, row_count, c_gate)
    ending = conv_grad[:, row_count - rim :].astype(jnp.float32) + rim_grad
    conv_grad = lax.dynamic_update_slice_in_dim(
        conv_grad, ending.astype(jnp.bfloat16), row_count - rim, 1
    ).reshape(total_rows, c_gate)
    late_grads = jnp.concatenate([conv_grad, step_grad], axis=1)
    late = t_dot(normed_one, late_grads).astype(jnp.bfloat16)
    late_width = late.shape[1] // 2 // SPAN * SPAN
    late_one, late_two, late_grads = tie(late[:, :late_width], late[:, late_width:], late_grads)
    late_one = scatter_stage(scatter_begin(late_one), "y")
    late_two = scatter_stage(scatter_begin(late_two), "x")
    normed_one_part = (
        early_part + dot_t(conv_grad, conv_all) + dot_t(step_grad, small_all[:, c_step - c_query :])
    )
    late_value, early_value, normed_one_part = tie(late_one[0], early[0], normed_one_part)
    late_one = scatter_stage((late_value, late_one[1]), "x")
    late_two = scatter_stage(late_two, "y")
    early = scatter_stage((early_value, early[1]), "z")
    normed_one_grad = sum_over(normed_one_part, "tp")
    late_total = jnp.concatenate(
        [scatter_end(scatter_stage(late_one, "z")), scatter_end(scatter_stage(late_two, "z"))], axis=1
    )
    early_total = scatter_end(early)
    first_back, first_gain_grad = norm_back(residual, first_inverse, first_gain, normed_one_grad)
    tokens_grad = (middle_grad + first_back).reshape(seq_count, row_count, model_width)

    state_table = sum_over(table_grad[:, inner_width:], "tp")
    flat = jnp.concatenate(
        [
            table_grad[:, :inner_width].reshape(-1),
            state_table.reshape(-1),
            gated_gain_grad,
            bias_grad,
            decay_log_grad,
            skip_grad,
        ]
    )
    flat_size = flat.shape[0]
    flat = jnp.pad(flat, (0, -flat_size % 1024)).reshape(-1, 128)
    for axis in WEIGHT_AXES:
        flat = sum_over(flat, axis)
    flat = flat.reshape(-1)
    tap_rows = conv_inner.shape[0]
    sizes = (
        tap_rows * inner_width,
        tap_rows * 2 * NS,
        inner_width,
        state_heads,
        state_heads,
        state_heads,
    )
    pieces, start = [], 0
    for size in sizes:
        pieces.append(flat[start : start + size])
        start += size
    conv_inner_total = pieces[0].reshape(tap_rows, inner_width)
    conv_state_total = pieces[1].reshape(tap_rows, 2 * NS)
    gated_total, bias_total, decay_total, skip_total = pieces[2:6]
    gain_total = jnp.stack([scatter_gain(first_gain_grad), scatter_gain(second_gain_grad)])

    wide_two = feed_total.astype(jnp.float32)
    mixer_total = jnp.stack(
        [
            early_total[:, :inner_width].reshape(own_rows, state_heads, MP),
            late_total[:, :inner_width].reshape(own_rows, state_heads, MP),
        ],
        axis=2,
    ).reshape(own_rows, state_heads, 2 * MP)
    state_weight_total = sum_over(late_total[:, c_state:c_gate], "tp")
    return (
        out_block,
        tokens_grad,
        gain_total,
        early_total[:, inner_width : inner_width + query_width],
        early_total[:, inner_width + query_width :].reshape(own_rows, 1, 2 * HEAD_DIMENSION),
        mix_total[:, inner_width:].T,
        mixer_total,
        state_weight_total,
        late_total[:, c_gate : c_gate + state_heads],
        conv_inner_total,
        conv_state_total,
        bias_total,
        decay_total,
        skip_total,
        gated_total,
        mix_total[:, :inner_width].T,
        wide_two[:, : 2 * hidden].reshape(own_rows, 2, hidden),
        wide_two[:, 2 * hidden : 3 * hidden].T,
    )


def solution(mesh):
    in_specs = (
        P("fsdp", "ctx", None),
        P("fsdp", "ctx", None),
        P(None, ("fsdp", "ctx")),
        P(("fsdp", "ctx"), "tp"),
        P(("fsdp", "ctx"), "tp", None),
        P("tp", ("fsdp", "ctx")),
        P(("fsdp", "ctx"), "tp", None),
        P(("fsdp", "ctx"), None),
        P(("fsdp", "ctx"), "tp"),
        P(None, "tp"),
        P(),
        P("tp"),
        P("tp"),
        P("tp"),
        P("tp"),
        P("tp", ("fsdp", "ctx")),
        P(("fsdp", "ctx"), None, "tp"),
        P("tp", ("fsdp", "ctx")),
    )
    out_specs = (
        P("fsdp", "ctx", "tp"),
        P("fsdp", "ctx", None),
        P(None, ("fsdp", "ctx")),
        P(("fsdp", "ctx"), "tp"),
        P(("fsdp", "ctx"), "tp", None),
        P("tp", ("fsdp", "ctx")),
        P(("fsdp", "ctx"), "tp", None),
        P(("fsdp", "ctx"), None),
        P(("fsdp", "ctx"), "tp"),
        P(None, "tp"),
        P(),
        P("tp"),
        P("tp"),
        P("tp"),
        P("tp"),
        P("tp", ("fsdp", "ctx")),
        P(("fsdp", "ctx"), None, "tp"),
        P("tp", ("fsdp", "ctx")),
    )
    return jax.shard_map(shards, mesh=mesh, in_specs=in_specs, out_specs=out_specs, check_vma=False)
```
